32 devices in a mesh: group: 2 (over x), chan: 16 (over z, y, core).
Axes of the slice: x: 2, y: 2, z: 4, core: 2. Of those that a mesh axis runs over, the one named last changes fastest.
Arguments:
- voltages: bfloat16 [32, 2, 256, 1024], P(('group', 'chan')), parts along dimension 0, may hold values from -6 to 6
- cal_num: float32 [32, 4, 512], P(('group', 'chan')), parts along dimension 0, may hold values from -6 to 6
- cal_weight: float32 [32, 2, 512], P(('group', 'chan')), parts along dimension 0, may hold values from 0.2 to 5
- flags: int32 [32, 512], P(('group', 'chan')), parts along dimension 0, may hold values 0 or 1
- positions: float32 [2, 512], replicated, may hold values from -300 to 300
- directions: float32 [2, 1024], replicated, may hold values from -0.05 to 0.05
- pointing: int32 [2048], P('group'), parts along dimension 0, may hold values from 0 to 1023, each once
Outputs:
- beam_power: bfloat16 [2048, 16, 128], P(('group', 'chan')), parts along dimension 0
- solved_gains: float32 [32, 4, 512], P(('group', 'chan')), parts along dimension 0
The draws below stay inside these ranges and needn't reach their ends.
There are 2 independent parts, one for each index of `group`. The reference program is written for one: setup_inputs(seed, part) draws one part's arguments, and reference() takes and returns one part's arrays. A program takes and returns all parts, laid end to end along the dimension named above; an argument that names none is the same for every part. Nothing has to cross between parts.
Inputs may be any that keep to these rules, and one draw needn't show every extreme that they name: `pointing`: each table direction is named by exactly one beam.
All inputs are finite; a program needn't handle non-finite values. No bound on the sum of `flags` on one device may be relied on, other than what follows from the above.
Results may differ from the reference program's by a relative error of at most 0.004.
Values may be sent and summed in bfloat16 or wider, within the bound.
No kernel may reach another device: no remote copies, remote signals or barrier semaphores. Data moves between devices by JAX's collectives and lax.ppermute only.
A program may use at most 64 MiB of HBM per device.

```python
import math
import jax
import jax.numpy as jnp
from jax import lax

S = 512
BEAMS = 1024
NDIR = 1024
K = 4
ITERS = 8
TIME = 256
CHANNELS = 16


def set_ends(entries, stream_key, low, top_value):
    index_at = [jax.random.randint(jax.random.fold_in(stream_key, axis), (), 0, length) for axis, length in enumerate(entries.shape)]
    longest = entries.shape.index(max(entries.shape))
    beside = index_at[:longest] + [(index_at[longest] + 1) % entries.shape[longest]] + index_at[longest + 1:]
    return entries.at[tuple(index_at)].set(low).at[tuple(beside)].set(top_value)


def levels(own_key, shape, cuts, low, largest):
    def one(axis_at, parts):
        heights = jax.random.uniform(jax.random.fold_in(jax.random.fold_in(own_key, 6), axis_at), (parts,), jnp.float32, low / len(cuts), largest / len(cuts))
        return jnp.repeat(jnp.exp(heights), shape[axis_at] // parts).reshape((-1,) + (1,) * (len(shape) - axis_at - 1))

    level = one(*cuts[0])
    for cut in cuts[1:]:
        level = level * one(*cut)
    return level


def gaussian(key, dims, scale, most, pieces=(), kind=jnp.bfloat16):
    result = scale * jax.random.normal(key, dims, jnp.float32)
    if pieces:
        result = result * levels(key, dims, pieces, -0.22, 0.18)
    return jnp.clip(result, -most, most).astype(kind)


def setup_inputs(seed: int = 0, part: int = 0) -> dict:
    streams_of = jax.random.split(jax.random.key(seed), 8)
    part_keys = jax.random.split(jax.random.fold_in(streams_of[7], part), 8)
    return {
        "voltages": gaussian(part_keys[0], (CHANNELS, 2, TIME, 2 * S), 1.0, 6.0, ((0, 16),)),
        "cal_num": gaussian(part_keys[1], (CHANNELS, 4, S), 1.0, 6.0, ((0, 16),), jnp.float32),
        "cal_weight": jnp.clip(jnp.exp(math.log(5.0) - 3.218876 * jax.random.uniform(part_keys[2], (CHANNELS, 2, S), jnp.float32) ** levels(part_keys[2], (CHANNELS, 2, S), ((0, 16),), -0.2, 0.2)), 0.2, 5.0),
        "flags": set_ends((jax.random.randint(part_keys[3], (CHANNELS, S), 0, 8) < 7).astype(jnp.int32), jax.random.fold_in(part_keys[3], 1), 0, 1),
        "positions": jnp.clip(jax.random.uniform(streams_of[4], (2, S), jnp.float32, -300.0, 300.0), -300.0, 300.0),
        "directions": jnp.clip(jax.random.uniform(streams_of[5], (2, NDIR), jnp.float32, -0.05, 0.05), -0.05, 0.05),
        "pointing": jax.random.permutation(part_keys[6], BEAMS).astype(jnp.int32),
    }


PENALTY = 2.0
RIDGE = 1.0
TWO_PI = 6.283185307179586
HIGHEST = lax.Precision.HIGHEST


def basis_rows(channel_ids, total):
    place = 2.0 * (channel_ids.astype(jnp.float32) + 0.5) / total - 1.0
    return jnp.stack([jnp.ones_like(place), place, 0.5 * (3.0 * place * place - 1.0), 0.5 * (5.0 * place * place * place - 3.0 * place)], axis=1)


def invert_small(matrix):
    order = matrix.shape[0]
    unit = jnp.ones_like(matrix[0, 0])
    nothing = jnp.zeros_like(matrix[0, 0])
    left = [[matrix[row, column] for column in range(order)] for row in range(order)]
    right = [[unit if row == column else nothing for column in range(order)] for row in range(order)]
    for pivot in range(order):
        factor = 1.0 / left[pivot][pivot]
        left[pivot] = [entry * factor for entry in left[pivot]]
        right[pivot] = [entry * factor for entry in right[pivot]]
        for row in range(order):
            if row != pivot:
                scale = left[row][pivot]
                left[row] = [first - scale * second for first, second in zip(left[row], left[pivot])]
                right[row] = [first - scale * second for first, second in zip(right[row], right[pivot])]
    return jnp.stack([jnp.stack(line, 0) for line in right], 0)


def beam_detect(volts, fitted, usable, ratio, projected):
    phase = projected * (TWO_PI * ratio)
    cosine = jnp.cos(phase)
    sine = jnp.sin(phase)
    stations = projected.shape[1]
    beams = projected.shape[0]
    scale = usable * (stations ** -0.5)
    total = jnp.zeros((beams, volts.shape[1]), jnp.float32)
    for polar in range(2):
        gain_re = (fitted[2 * polar] * scale)[None, :]
        gain_im = (fitted[2 * polar + 1] * scale)[None, :]
        w_re = (gain_re * cosine - gain_im * sine).astype(jnp.bfloat16)
        w_im = (-(gain_re * sine + gain_im * cosine)).astype(jnp.bfloat16)
        upper = jnp.concatenate([w_re, -w_im], axis=1)
        lower = jnp.concatenate([w_im, w_re], axis=1)
        matrix = jnp.concatenate([upper, lower], axis=0)
        output = lax.dot_general(matrix, volts[polar], (((1,), (1,)), ((), ())), preferred_element_type=jnp.float32)
        total = total + output[:beams] * output[:beams] + output[beams:] * output[beams:]
    return total


def reference(voltages, cal_num, cal_weight, flags, positions, directions, pointing):
    channel_ids = jnp.arange(CHANNELS, dtype=jnp.int32)
    basis = basis_rows(channel_ids, CHANNELS)
    usable = flags.astype(jnp.float32)
    gram = jnp.einsum("ck,cj,cs->kjs", basis, basis, usable, precision=HIGHEST)
    identity = jnp.eye(K, dtype=jnp.float32)[:, :, None]
    inverse = invert_small(gram + RIDGE * identity)
    weight4 = jnp.repeat(cal_weight, 2, axis=1)
    mask = usable[:, None, :]
    fitted = jnp.zeros(cal_num.shape, jnp.float32)
    dual = jnp.zeros(cal_num.shape, jnp.float32)
    for sweep in range(ITERS):
        local = (mask * cal_num + PENALTY * (fitted - dual)) / (mask * weight4 + PENALTY)
        numerator = jnp.einsum("ck,cqs->kqs", basis, mask * (local + dual), precision=HIGHEST)
        coefficients = jnp.einsum("kjs,jqs->kqs", inverse, numerator, precision=HIGHEST)
        fitted = jnp.einsum("ck,kqs->cqs", basis, coefficients, precision=HIGHEST)
        dual = dual + mask * (local - fitted)
    east = directions[0][pointing]
    north = directions[1][pointing]
    projected = east[:, None] * positions[0][None, :] + north[:, None] * positions[1][None, :]
    ratio = 1.0 + 0.3 * (channel_ids.astype(jnp.float32) + 0.5) / CHANNELS

    def one_channel(items):
        volts, fit_one, usable_one, ratio_one = items
        power = beam_detect(volts, fit_one, usable_one, ratio_one, projected)
        return ((power[:, 0::2] + power[:, 1::2]) * 0.5).astype(jnp.bfloat16)

    detected = lax.map(one_channel, (voltages, fitted, usable, ratio))
    beam_power = jnp.transpose(detected, (1, 0, 2))
    return beam_power, fitted
```

```python
import functools

import jax
import jax.numpy as jnp
import numpy as np
from jax import lax
from jax.experimental import pallas as pl
from jax.experimental.pallas import tpu as pltpu
from jax.sharding import PartitionSpec as P

ITERS = 8
ORDER = 4
PENALTY = 2.0
RIDGE = 1.0
VMEM = pltpu.VMEM
MIB = 1 << 20


def legendre(place):
    return [
        1.0,
        place,
        0.5 * (3.0 * place * place - 1.0),
        0.5 * (5.0 * place * place * place - 3.0 * place),
    ]


def basis_table(total):
    place = np.float32(2.0) * (np.arange(total, dtype=np.float32) + np.float32(0.5)) / np.float32(
        total
    ) - np.float32(1.0)
    return np.stack([np.broadcast_to(np.float32(v), place.shape) for v in legendre(place)], 1)


def whole(shape_count):
    return [pl.BlockSpec(memory_space=VMEM)] * shape_count


def pack_kernel(num_ref, weight_ref, flag_ref, out_ref):
    half = num_ref.shape[1] // 2
    mask = flag_ref[...].astype(jnp.float32)
    num = num_ref[...] * mask
    weight = weight_ref[...] * mask
    weight4 = jnp.concatenate([weight[0:1], weight[0:1], weight[1:2], weight[1:2]], 0)
    block = jnp.concatenate(
        [num[:, :half], num[:, half:], weight4[:, :half], weight4[:, half:]], 0
    )
    for peer in range(out_ref.shape[0]):
        out_ref[peer] = block


def pack(cal_num, cal_weight, flags, devices):
    stations = cal_num.shape[1]
    return pl.pallas_call(
        pack_kernel,
        out_shape=jax.ShapeDtypeStruct((devices, 16, stations // 2), jnp.float32),
        in_specs=whole(3),
        out_specs=pl.BlockSpec(memory_space=VMEM),
        compiler_params=pltpu.CompilerParams(vmem_limit_bytes=8 * MIB),
        name="pack",
    )(cal_num, cal_weight, flags)


def fit_polynomials():
    nodes = np.cos(np.pi * (np.arange(400) + 0.5) / 400) * 0.5
    square = nodes * nodes
    safe = np.sinc(nodes) * np.pi
    sine = np.polynomial.chebyshev.Chebyshev.fit(square, safe, 5, domain=[0, 0.25])
    cosine = np.polynomial.chebyshev.Chebyshev.fit(square, np.cos(np.pi * nodes), 5, domain=[0, 0.25])
    to_power = lambda c: c.convert(kind=np.polynomial.Polynomial).coef
    return [float(np.float32(v)) for v in to_power(sine)], [
        float(np.float32(v)) for v in to_power(cosine)
    ]


def horner(coefficients, x):
    value = coefficients[-1]
    for c in coefficients[-2::-1]:
        value = value * x + c
    return value


def phasor_kernel(rows, total, volts_ref, pos_ref, dir_ref, point_ref, cos_ref, sin_ref, rhs_ref, dirs):
    table = dir_ref.shape[1]
    beams = point_ref.shape[1]
    stations = pos_ref.shape[1]
    samples = volts_ref.shape[1]
    channel = lax.axis_index("chan").astype(jnp.float32)
    ratio = 1.0 + 0.3 * (channel + 0.5) / total

    d = dir_ref[...]
    high = d.astype(jnp.bfloat16)
    rest = d - high.astype(jnp.float32)
    middle = rest.astype(jnp.bfloat16)
    low = (rest - middle.astype(jnp.float32)).astype(jnp.bfloat16)
    zero = jnp.zeros_like(d)
    parts = jnp.concatenate(
        [high.astype(jnp.float32), middle.astype(jnp.float32), low.astype(jnp.float32), zero], 0
    ).astype(jnp.bfloat16)
    hot = (
        lax.broadcasted_iota(jnp.int32, (table, beams), 0) == point_ref[...]
    ).astype(jnp.float32).astype(jnp.bfloat16)
    found = jnp.dot(parts, hot, preferred_element_type=jnp.float32)
    exact = found[0:2] + found[2:4] + found[4:6]
    dirs[...] = jnp.transpose(jnp.concatenate([exact, exact, exact, exact], 0))

    half = samples // 2
    row = lax.broadcasted_iota(jnp.int32, (samples, samples), 0)
    column = lax.broadcasted_iota(jnp.int32, (samples, samples), 1)
    source = jnp.where(column < half, 2 * column, 2 * (column - half) + 1)
    spread = (row == source).astype(jnp.float32).astype(jnp.bfloat16)
    for polar in range(2):
        turned = lax.dot_general(
            volts_ref[polar], spread, (((0,), (0,)), ((), ())), preferred_element_type=jnp.float32
        )
        real, imag = turned[:stations], turned[stations:]
        rhs_ref[polar, :stations, :samples] = real.astype(jnp.bfloat16)
        rhs_ref[polar, stations:, :samples] = (-imag).astype(jnp.bfloat16)
        rhs_ref[polar, :stations, samples:] = imag.astype(jnp.bfloat16)
        rhs_ref[polar, stations:, samples:] = real.astype(jnp.bfloat16)

    sine_c, cosine_c = fit_polynomials()
    east = pos_ref[0:1, :] * ratio
    north = pos_ref[1:2, :] * ratio

    @pl.loop(0, beams // rows)
    def _(step):
        at = pl.ds(pl.multiple_of(step * rows, rows), rows)
        l = dirs[at, 0:1]
        m = dirs[at, 1:2]
        turns = l * east + m * north
        x = turns - jnp.round(turns)
        square = x * x
        s = x * horner(sine_c, square)
        c = horner(cosine_c, square)
        cos_ref[at, :] = 1.0 - 2.0 * (s * s)
        sin_ref[at, :] = 2.0 * (s * c)


def phasors(volts, positions, directions, pointing, total):
    beams = pointing.shape[1]
    stations = positions.shape[1]
    samples = volts.shape[1]
    return pl.pallas_call(
        functools.partial(phasor_kernel, 16, total),
        out_shape=(
            jax.ShapeDtypeStruct((beams, stations), jnp.float32),
            jax.ShapeDtypeStruct((beams, stations), jnp.float32),
            jax.ShapeDtypeStruct((2, 2 * stations, 2 * samples), jnp.bfloat16),
        ),
        in_specs=whole(4),
        out_specs=tuple(whole(3)),
        scratch_shapes=[pltpu.VMEM((beams, 8), jnp.float32)],
        compiler_params=pltpu.CompilerParams(vmem_limit_bytes=32 * MIB),
        cost_estimate=pl.CostEstimate(
            flops=60 * beams * stations, bytes_accessed=8 * MIB, transcendentals=0
        ),
        name="phasors",
    )(volts, positions, directions, pointing)


def invert_small(left):
    order = len(left)
    unit = jnp.ones_like(left[0][0])
    nothing = jnp.zeros_like(unit)
    right = [[unit if r == c else nothing for c in range(order)] for r in range(order)]
    for pivot in range(order):
        factor = 1.0 / left[pivot][pivot]
        left[pivot] = [entry * factor for entry in left[pivot]]
        right[pivot] = [entry * factor for entry in right[pivot]]
        for r in range(order):
            if r != pivot:
                scale = left[r][pivot]
                left[r] = [a - scale * b for a, b in zip(left[r], left[pivot])]
                right[r] = [a - scale * b for a, b in zip(right[r], right[pivot])]
    return right


def combine(weights, values):
    total = None
    for w, v in zip(weights, values):
        term = v if isinstance(w, float) and w == 1.0 else w * v
        total = term if total is None else total + term
    return total


def fit_kernel(cal_ref, out_ref, target, gain, mask_ref, dual, local):
    total = cal_ref.shape[0]
    half = cal_ref.shape[2]
    table = basis_table(total)
    rows = [[float(v) for v in line] for line in table]

    gram = [[None] * ORDER for _ in range(ORDER)]
    for c in range(total):
        weight = cal_ref[c, 8:16, :]
        mask = jnp.where(weight > 0.0, 1.0, 0.0)
        inverse = mask / (weight + PENALTY)
        target[c] = cal_ref[c, 0:8, :] * inverse
        gain[c] = PENALTY * inverse
        mask_ref[c] = mask
        dual[c] = jnp.zeros_like(mask)
        local[c] = jnp.zeros_like(mask)
        for k in range(ORDER):
            for j in range(k, ORDER):
                term = mask * (rows[c][k] * rows[c][j])
                gram[k][j] = term if gram[k][j] is None else gram[k][j] + term
    for k in range(ORDER):
        gram[k][k] = gram[k][k] + RIDGE
        for j in range(k):
            gram[k][j] = gram[j][k]
    inverse = invert_small(gram)

    def sweep(_, coefficients):
        sums = [None] * ORDER
        for c in range(total):
            fitted = combine(rows[c], coefficients)
            mask = mask_ref[c]
            d = dual[c] + (local[c] - mask * fitted)
            new = target[c] + gain[c] * (fitted - d)
            dual[c] = d
            local[c] = new
            u = new + d
            for k in range(ORDER):
                term = u if rows[c][k] == 1.0 else rows[c][k] * u
                sums[k] = term if sums[k] is None else sums[k] + term
        return tuple(combine(inverse[k], sums) for k in range(ORDER))

    zero = jnp.zeros((8, half), jnp.float32)
    coefficients = lax.fori_loop(0, ITERS, sweep, (zero,) * ORDER)
    channel = lax.axis_index("chan").astype(jnp.float32)
    place = 2.0 * (channel + 0.5) / total - 1.0
    fitted = combine(legendre(place), coefficients)
    out_ref[:, :half] = fitted[0:4]
    out_ref[:, half:] = fitted[4:8]


def fit(cal):
    total, _, half = cal.shape
    block = pltpu.VMEM((total, 8, half), jnp.float32)
    return pl.pallas_call(
        fit_kernel,
        out_shape=jax.ShapeDtypeStruct((4, 2 * half), jnp.float32),
        in_specs=whole(1),
        out_specs=pl.BlockSpec(memory_space=VMEM),
        scratch_shapes=[block] * 5,
        compiler_params=pltpu.CompilerParams(vmem_limit_bytes=16 * MIB),
        name="fit",
    )(cal)


def beam_kernel(fitted_ref, flag_ref, cos_ref, sin_ref, rhs_ref, out_ref):
    stations = cos_ref.shape[1]
    samples = rhs_ref.shape[2] // 2
    half = samples // 2
    scale = flag_ref[...].astype(jnp.float32) * stations ** (-0.5)
    gains = fitted_ref[...] * scale
    cosine = cos_ref[...]
    sine = sin_ref[...]
    power = None
    for polar in range(2):
        re = gains[2 * polar : 2 * polar + 1]
        im = gains[2 * polar + 1 : 2 * polar + 2]
        w_re = (re * cosine - im * sine).astype(jnp.bfloat16)
        w_im = (-(re * sine + im * cosine)).astype(jnp.bfloat16)
        lhs = jnp.concatenate([w_re, w_im], 1)
        y = jnp.dot(lhs, rhs_ref[polar], preferred_element_type=jnp.float32)
        y = y * y
        y = y[:, :samples] + y[:, samples:]
        power = y if power is None else power + y
    out_ref[...] = ((power[:, :half] + power[:, half:]) * 0.5).astype(jnp.bfloat16)


def beams_detect(fitted, flags, cosine, sine, rhs, rows):
    beams, stations = cosine.shape
    samples = rhs.shape[2] // 2
    fixed = lambda *shape: pl.BlockSpec(shape, lambda i: (0,) * len(shape))
    return pl.pallas_call(
        beam_kernel,
        grid=(beams // rows,),
        out_shape=jax.ShapeDtypeStruct((beams, samples // 2), jnp.bfloat16),
        in_specs=[
            fixed(4, stations),
            fixed(1, stations),
            pl.BlockSpec((rows, stations), lambda i: (i, 0)),
            pl.BlockSpec((rows, stations), lambda i: (i, 0)),
            fixed(2, 2 * stations, 2 * samples),
        ],
        out_specs=pl.BlockSpec((rows, samples // 2), lambda i: (i, 0)),
        compiler_params=pltpu.CompilerParams(vmem_limit_bytes=32 * MIB),
        name="beams",
    )(fitted, flags, cosine, sine, rhs)


def body(voltages, cal_num, cal_weight, flags, positions, directions, pointing):
    devices = lax.axis_size("chan")
    assert voltages.shape[0] == 1
    total = devices
    packed = pack(cal_num[0], cal_weight[0], flags, devices)
    cal = lax.all_to_all(packed, "chan", 0, 0, tiled=True)
    cosine, sine, rhs = phasors(voltages[0], positions, directions, pointing[None, :], total)
    fitted = fit(cal)
    power = beams_detect(fitted, flags, cosine, sine, rhs, 256)
    moved = lax.all_to_all(power, "chan", 0, 0, tiled=True)
    beams = power.shape[0] // devices
    beam_power = jnp.transpose(moved.reshape(devices, beams, power.shape[1]), (1, 0, 2))
    return beam_power, fitted[None]


def solution(mesh):
    return jax.shard_map(
        body,
        mesh=mesh,
        in_specs=(
            P(("group", "chan"), None, None, None),
            P(("group", "chan"), None, None),
            P(("group", "chan"), None, None),
            P(("group", "chan"), None),
            P(),
            P(),
            P("group"),
        ),
        out_specs=(P(("group", "chan"), None, None), P(("group", "chan"), None, None)),
        check_vma=False,
    )
```

```python
import functools

import jax
import jax.numpy as jnp
import numpy as np
from jax import lax
from jax.experimental import pallas as pl
from jax.experimental.pallas import tpu as pltpu
from jax.sharding import PartitionSpec as P

ITERS = 8
ORDER = 4
PENALTY = 2.0
RIDGE = 1.0
MIB = 1 << 20
GRANT = 67_000_000


def legendre(place):
    return [
        1.0,
        place,
        0.5 * (3.0 * place * place - 1.0),
        0.5 * (5.0 * place * place * place - 3.0 * place),
    ]


def basis_table(total):
    place = np.float32(2.0) * (np.arange(total, dtype=np.float32) + np.float32(0.5)) / np.float32(
        total
    ) - np.float32(1.0)
    return np.stack([np.broadcast_to(np.float32(v), place.shape) for v in legendre(place)], 1)


HBM_SPEC = pl.BlockSpec(memory_space=pltpu.HBM)
VMEM_SPEC = pl.BlockSpec(memory_space=pltpu.VMEM)


def start(source, target, semaphore):
    copy = pltpu.make_async_copy(source, target, semaphore)
    copy.start()
    return copy


def pack_kernel(num_hbm, weight_hbm, flag_hbm, out_ref, num_ref, weight_ref, flag_ref, sems):
    copies = [
        start(num_hbm, num_ref, sems.at[0]),
        start(weight_hbm, weight_ref, sems.at[1]),
        start(flag_hbm, flag_ref, sems.at[2]),
    ]
    for copy in copies:
        copy.wait()
    half = num_ref.shape[1] // 2
    mask = flag_ref[...].astype(jnp.float32)
    num = num_ref[...] * mask
    weight = weight_ref[...] * mask
    weight4 = jnp.concatenate([weight[0:1], weight[0:1], weight[1:2], weight[1:2]], 0)
    block = jnp.concatenate(
        [num[:, :half], num[:, half:], weight4[:, :half], weight4[:, half:]], 0
    )
    for peer in range(out_ref.shape[0]):
        out_ref[peer] = block


def pack(cal_num, cal_weight, flags, devices):
    stations = cal_num.shape[1]
    return pl.pallas_call(
        pack_kernel,
        out_shape=jax.ShapeDtypeStruct((devices, 16, stations // 2), jnp.float32),
        in_specs=[HBM_SPEC] * 3,
        out_specs=VMEM_SPEC,
        scratch_shapes=[
            pltpu.VMEM(cal_num.shape, jnp.float32),
            pltpu.VMEM(cal_weight.shape, jnp.float32),
            pltpu.VMEM(flags.shape, jnp.int32),
            pltpu.SemaphoreType.DMA((3,)),
        ],
        compiler_params=pltpu.CompilerParams(vmem_limit_bytes=GRANT),
        name="pack",
    )(cal_num, cal_weight, flags)


def fit_polynomials():
    nodes = np.cos(np.pi * (np.arange(400) + 0.5) / 400) * 0.5
    square = nodes * nodes
    safe = np.sinc(nodes) * np.pi
    chebyshev = np.polynomial.chebyshev.Chebyshev
    sine = chebyshev.fit(square, safe, 4, domain=[0, 0.25])
    cosine = chebyshev.fit(square, np.cos(np.pi * nodes), 5, domain=[0, 0.25])
    to_power = lambda c: c.convert(kind=np.polynomial.Polynomial).coef * np.sqrt(2.0)
    return [float(np.float32(v)) for v in to_power(sine)], [
        float(np.float32(v)) for v in to_power(cosine)
    ]


def horner(coefficients, x):
    value = coefficients[-1]
    for c in coefficients[-2::-1]:
        value = value * x + c
    return value


def phasor_kernel(
    rows, blocks, total, volts_hbm, pos_hbm, dir_hbm, point_hbm, phase_hbm, rhs_hbm,
    volts_ref, pos_ref, dir_ref, point_ref, phase_ref, rhs_ref, dirs, sems, out_sems,
):
    incoming = [
        start(point_hbm, point_ref, sems.at[0]),
        start(dir_hbm, dir_ref, sems.at[1]),
        start(pos_hbm, pos_ref, sems.at[2]),
        start(volts_hbm, volts_ref, sems.at[3]),
    ]
    table = dir_ref.shape[1]
    beams = point_ref.shape[1]
    stations = pos_ref.shape[1]
    samples = volts_ref.shape[1]
    channel = lax.axis_index("chan").astype(jnp.float32)
    ratio = 1.0 + 0.3 * (channel + 0.5) / total
    for copy in incoming[:3]:
        copy.wait()

    d = dir_ref[...]
    high = d.astype(jnp.bfloat16).astype(jnp.float32)
    middle = (d - high).astype(jnp.bfloat16).astype(jnp.float32)
    low = d - high - middle
    parts = jnp.concatenate([high, middle, low, jnp.zeros_like(d)], 0).astype(jnp.bfloat16)
    hot = (
        (lax.broadcasted_iota(jnp.int32, (table, beams), 0) == point_ref[...])
        .astype(jnp.float32)
        .astype(jnp.bfloat16)
    )
    found = jnp.dot(parts, hot, preferred_element_type=jnp.float32)
    exact = found[0:2] + found[2:4] + found[4:6]
    dirs[...] = jnp.transpose(jnp.concatenate([exact] * 4, 0))

    sine_c, cosine_c = fit_polynomials()
    east = pos_ref[0:1, :] * ratio
    north = pos_ref[1:2, :] * ratio
    magic = 12582912.0
    per_block = beams // blocks
    outgoing = []
    for block in range(blocks):

        @pl.loop(0, per_block // rows, unroll=2)
        def _(step):
            at = pl.ds(pl.multiple_of(block * per_block + step * rows, rows), rows)
            turns = dirs[at, 0:1] * east + dirs[at, 1:2] * north
            x = turns - ((turns + magic) - magic)
            square = x * x
            s = x * horner(sine_c, square)
            c = horner(cosine_c, square)
            phase_ref[0, at, :] = 1.0 - s * s
            phase_ref[1, at, :] = s * c

        part = pl.ds(block * per_block, per_block)
        outgoing.append(start(phase_ref.at[:, part], phase_hbm.at[:, part], out_sems.at[block]))

    incoming[3].wait()
    half = samples // 2
    row = lax.broadcasted_iota(jnp.int32, (samples, samples), 0)
    column = lax.broadcasted_iota(jnp.int32, (samples, samples), 1)
    source = jnp.where(column < half, 2 * column, 2 * (column - half) + 1)
    spread = (row == source).astype(jnp.float32).astype(jnp.bfloat16)
    for polar in range(2):
        turned = lax.dot_general(
            volts_ref[polar], spread, (((0,), (0,)), ((), ())), preferred_element_type=jnp.float32
        )
        real, imag = turned[:stations], turned[stations:]
        rhs_ref[polar, :stations, :samples] = real.astype(jnp.bfloat16)
        rhs_ref[polar, stations:, :samples] = (-imag).astype(jnp.bfloat16)
        rhs_ref[polar, :stations, samples:] = imag.astype(jnp.bfloat16)
        rhs_ref[polar, stations:, samples:] = real.astype(jnp.bfloat16)
        outgoing.append(start(rhs_ref.at[polar], rhs_hbm.at[polar], out_sems.at[blocks + polar]))
    for copy in outgoing:
        copy.wait()


def phasors(volts, positions, directions, pointing, total):
    beams = pointing.shape[1]
    stations = positions.shape[1]
    samples = volts.shape[1]
    blocks = 4
    phase = (2, beams, stations)
    rhs = (2, 2 * stations, 2 * samples)
    return pl.pallas_call(
        functools.partial(phasor_kernel, 16, blocks, total),
        out_shape=(
            jax.ShapeDtypeStruct(phase, jnp.float32),
            jax.ShapeDtypeStruct(rhs, jnp.bfloat16),
        ),
        in_specs=[HBM_SPEC] * 4,
        out_specs=(HBM_SPEC, HBM_SPEC),
        scratch_shapes=[
            pltpu.VMEM(volts.shape, volts.dtype),
            pltpu.VMEM(positions.shape, jnp.float32),
            pltpu.VMEM(directions.shape, jnp.float32),
            pltpu.VMEM(pointing.shape, jnp.int32),
            pltpu.VMEM(phase, jnp.float32),
            pltpu.VMEM(rhs, jnp.bfloat16),
            pltpu.VMEM((beams, 8), jnp.float32),
            pltpu.SemaphoreType.DMA((4,)),
            pltpu.SemaphoreType.DMA((blocks + 2,)),
        ],
        compiler_params=pltpu.CompilerParams(vmem_limit_bytes=GRANT),
        cost_estimate=pl.CostEstimate(
            flops=60 * beams * stations, bytes_accessed=8 * MIB, transcendentals=0
        ),
        name="phasors",
    )(volts, positions, directions, pointing)


def invert_small(left):
    order = len(left)
    unit = jnp.ones_like(left[0][0])
    nothing = jnp.zeros_like(unit)
    right = [[unit if r == c else nothing for c in range(order)] for r in range(order)]
    for pivot in range(order):
        factor = 1.0 / left[pivot][pivot]
        left[pivot] = [entry * factor for entry in left[pivot]]
        right[pivot] = [entry * factor for entry in right[pivot]]
        for r in range(order):
            if r != pivot:
                scale = left[r][pivot]
                left[r] = [a - scale * b for a, b in zip(left[r], left[pivot])]
                right[r] = [a - scale * b for a, b in zip(right[r], right[pivot])]
    return right


def combine(weights, values):
    total = None
    for w, v in zip(weights, values):
        term = v if isinstance(w, float) and w == 1.0 else w * v
        total = term if total is None else total + term
    return total


def solve(cal_ref, target, gain, mask_ref, dual, local):
    total = cal_ref.shape[0]
    half = cal_ref.shape[2]
    rows = [[float(v) for v in line] for line in basis_table(total)]

    gram = [[None] * ORDER for _ in range(ORDER)]
    for c in range(total):
        weight = cal_ref[c, 8:16, :]
        mask = jnp.where(weight > 0.0, 1.0, 0.0)
        inverse = mask / (weight + PENALTY)
        target[c] = cal_ref[c, 0:8, :] * inverse
        gain[c] = PENALTY * inverse
        mask_ref[c] = mask
        dual[c] = jnp.zeros_like(mask)
        local[c] = jnp.zeros_like(mask)
        for k in range(ORDER):
            for j in range(k, ORDER):
                term = mask * (rows[c][k] * rows[c][j])
                gram[k][j] = term if gram[k][j] is None else gram[k][j] + term
    for k in range(ORDER):
        gram[k][k] = gram[k][k] + RIDGE
        for j in range(k):
            gram[k][j] = gram[j][k]
    inverse = invert_small(gram)

    def sweep(_, coefficients):
        sums = [None] * ORDER
        for c in range(total):
            fitted = combine(rows[c], coefficients)
            d = dual[c] + (local[c] - mask_ref[c] * fitted)
            new = target[c] + gain[c] * (fitted - d)
            dual[c] = d
            local[c] = new
            u = new + d
            for k in range(ORDER):
                term = u if rows[c][k] == 1.0 else rows[c][k] * u
                sums[k] = term if sums[k] is None else sums[k] + term
        return tuple(combine(inverse[k], sums) for k in range(ORDER))

    zero = jnp.zeros((8, half), jnp.float32)
    coefficients = lax.fori_loop(0, ITERS, sweep, (zero,) * ORDER)
    channel = lax.axis_index("chan").astype(jnp.float32)
    place = 2.0 * (channel + 0.5) / total - 1.0
    return combine(legendre(place), coefficients)


def beam_kernel(
    blocks, cal_ref, phase_hbm, rhs_hbm, out_ref, fitted_ref,
    phase_ref, rhs_ref, target, gain, mask_ref, dual, local, sems,
):
    stations = phase_ref.shape[2]
    samples = rhs_ref.shape[2] // 2
    half = samples // 2
    per_block = phase_ref.shape[1] // blocks
    rhs_copy = start(rhs_hbm, rhs_ref, sems.at[0])
    phase_copies = []
    for block in range(blocks):
        part = pl.ds(block * per_block, per_block)
        phase_copies.append(start(phase_hbm.at[:, part], phase_ref.at[:, part], sems.at[1 + block]))

    fitted = solve(cal_ref, target, gain, mask_ref, dual, local)
    fitted_ref[:, : stations // 2] = fitted[0:4]
    fitted_ref[:, stations // 2 :] = fitted[4:8]
    dense = fitted * (mask_ref[lax.axis_index("chan")] * stations ** (-0.5))
    gains = jnp.concatenate([dense[0:4], dense[4:8]], 1)
    rhs_copy.wait()
    for block in range(blocks):
        part = pl.ds(block * per_block, per_block)
        phase_copies[block].wait()
        cosine = phase_ref[0, part]
        sine = phase_ref[1, part]
        power = None
        for polar in range(2):
            re = gains[2 * polar : 2 * polar + 1]
            im = gains[2 * polar + 1 : 2 * polar + 2]
            w_re = (re * cosine - im * sine).astype(jnp.bfloat16)
            w_im = (-(re * sine + im * cosine)).astype(jnp.bfloat16)
            lhs = jnp.concatenate([w_re, w_im], 1)
            y = jnp.dot(lhs, rhs_ref[polar], preferred_element_type=jnp.float32)
            y = y * y
            y = y[:, :samples] + y[:, samples:]
            power = y if power is None else power + y
        out_ref[part, :] = ((power[:, :half] + power[:, half:]) * 0.5).astype(jnp.bfloat16)


def fit_and_detect(cal, phase, rhs):
    total, _, half_stations = cal.shape
    _, beams, stations = phase.shape
    samples = rhs.shape[2] // 2
    blocks = 4
    state = pltpu.VMEM((total, 8, half_stations), jnp.float32)
    return pl.pallas_call(
        functools.partial(beam_kernel, blocks),
        out_shape=(
            jax.ShapeDtypeStruct((beams, samples // 2), jnp.bfloat16),
            jax.ShapeDtypeStruct((4, stations), jnp.float32),
        ),
        in_specs=[VMEM_SPEC, HBM_SPEC, HBM_SPEC],
        out_specs=(VMEM_SPEC, VMEM_SPEC),
        scratch_shapes=[
            pltpu.VMEM(phase.shape, jnp.float32),
            pltpu.VMEM(rhs.shape, jnp.bfloat16),
        ]
        + [state] * 5
        + [pltpu.SemaphoreType.DMA((1 + blocks,))],
        compiler_params=pltpu.CompilerParams(vmem_limit_bytes=GRANT - MIB),
        name="beams",
    )(cal, phase, rhs)


def body(voltages, cal_num, cal_weight, flags, positions, directions, pointing):
    devices = lax.axis_size("chan")
    assert voltages.shape[0] == 1
    total = devices
    packed = pack(cal_num[0], cal_weight[0], flags, devices)
    cal = lax.all_to_all(packed, "chan", 0, 0, tiled=True)
    phase, rhs = phasors(voltages[0], positions, directions, pointing[None, :], total)
    power, fitted = fit_and_detect(cal, phase, rhs)
    moved = lax.all_to_all(power, "chan", 0, 0, tiled=True)
    beams = power.shape[0] // devices
    beam_power = jnp.transpose(moved.reshape(devices, beams, power.shape[1]), (1, 0, 2))
    return beam_power, fitted[None]


def solution(mesh):
    return jax.shard_map(
        body,
        mesh=mesh,
        in_specs=(
            P(("group", "chan"), None, None, None),
            P(("group", "chan"), None, None),
            P(("group", "chan"), None, None),
            P(("group", "chan"), None),
            P(),
            P(),
            P("group"),
        ),
        out_specs=(P(("group", "chan"), None, None), P(("group", "chan"), None, None)),
        check_vma=False,
    )
```

```python
import functools

import jax
import jax.numpy as jnp
import numpy as np
from jax import lax
from jax.experimental import pallas as pl
from jax.experimental.pallas import tpu as pltpu
from jax.sharding import PartitionSpec as P

ITERS = 8
ORDER = 4
PENALTY = 2.0
RIDGE = 1.0
MIB = 1 << 20
LANES = 128
GRANT = 67_000_000


def legendre(place):
    return [
        1.0,
        place,
        0.5 * (3.0 * place * place - 1.0),
        0.5 * (5.0 * place * place * place - 3.0 * place),
    ]


def basis_table(total):
    place = np.float32(2.0) * (np.arange(total, dtype=np.float32) + np.float32(0.5)) / np.float32(
        total
    ) - np.float32(1.0)
    return np.stack([np.broadcast_to(np.float32(v), place.shape) for v in legendre(place)], 1)


HBM_SPEC = pl.BlockSpec(memory_space=pltpu.HBM)
VMEM_SPEC = pl.BlockSpec(memory_space=pltpu.VMEM)


def start(source, target, semaphore):
    copy = pltpu.make_async_copy(source, target, semaphore)
    copy.start()
    return copy


def pack_kernel(num_hbm, weight_hbm, flag_hbm, out_ref, num_ref, weight_ref, flag_ref, sems):
    copies = [
        start(num_hbm, num_ref, sems.at[0]),
        start(weight_hbm, weight_ref, sems.at[1]),
        start(flag_hbm, flag_ref, sems.at[2]),
    ]
    for copy in copies:
        copy.wait()
    half = num_ref.shape[1] // 2
    mask = flag_ref[...].astype(jnp.float32)
    num = num_ref[...] * mask
    weight = weight_ref[...] * mask
    weight4 = jnp.concatenate([weight[0:1], weight[0:1], weight[1:2], weight[1:2]], 0)
    block = jnp.concatenate(
        [num[:, :half], num[:, half:], weight4[:, :half], weight4[:, half:]], 0
    ).astype(out_ref.dtype)
    for peer in range(out_ref.shape[0]):
        out_ref[peer] = block


def pack(cal_num, cal_weight, flags, devices):
    stations = cal_num.shape[1]
    return pl.pallas_call(
        pack_kernel,
        out_shape=jax.ShapeDtypeStruct((devices, 16, stations // 2), jnp.bfloat16),
        in_specs=[HBM_SPEC] * 3,
        out_specs=VMEM_SPEC,
        scratch_shapes=[
            pltpu.VMEM(cal_num.shape, jnp.float32),
            pltpu.VMEM(cal_weight.shape, jnp.float32),
            pltpu.VMEM(flags.shape, jnp.int32),
            pltpu.SemaphoreType.DMA((3,)),
        ],
        compiler_params=pltpu.CompilerParams(vmem_limit_bytes=GRANT),
        name="pack",
    )(cal_num, cal_weight, flags)


def fit_polynomials():
    nodes = np.cos(np.pi * (np.arange(400) + 0.5) / 400) * 0.5
    square = nodes * nodes
    safe = np.sinc(nodes) * np.pi
    chebyshev = np.polynomial.chebyshev.Chebyshev
    sine = chebyshev.fit(square, safe, 4, domain=[0, 0.25])
    cosine = chebyshev.fit(square, np.cos(np.pi * nodes), 5, domain=[0, 0.25])
    to_power = lambda c: c.convert(kind=np.polynomial.Polynomial).coef * np.sqrt(2.0)
    return [float(np.float32(v)) for v in to_power(sine)], [
        float(np.float32(v)) for v in to_power(cosine)
    ]


def horner(coefficients, x):
    value = coefficients[-1]
    for c in coefficients[-2::-1]:
        value = value * x + c
    return value


def thirds(x):
    high = x.astype(jnp.bfloat16).astype(jnp.float32)
    middle = (x - high).astype(jnp.bfloat16).astype(jnp.float32)
    return [high, middle, x - high - middle]


def phasor_kernel(
    rows, blocks, total, volts_hbm, pos_hbm, dir_hbm, point_hbm, phase_hbm, rhs_hbm,
    volts_ref, pos_ref, dir_ref, point_ref, phase_ref, rhs_ref, dirs, sems, out_sems,
):
    incoming = [
        start(point_hbm, point_ref, sems.at[0]),
        start(dir_hbm, dir_ref, sems.at[1]),
        start(pos_hbm, pos_ref, sems.at[2]),
        start(volts_hbm, volts_ref, sems.at[3]),
    ]
    table = dir_ref.shape[1]
    beams = point_ref.shape[1]
    stations = pos_ref.shape[1]
    samples = volts_ref.shape[1]
    channel = lax.axis_index("chan").astype(jnp.float32)
    ratio = 1.0 + 0.3 * (channel + 0.5) / total
    for copy in incoming[:3]:
        copy.wait()

    parts = jnp.concatenate(thirds(dir_ref[...]) + [jnp.zeros_like(dir_ref[...])], 0)
    groups = table // LANES
    stack = jnp.concatenate([parts[:, g * LANES : (g + 1) * LANES] for g in range(groups)], 0)
    point = point_ref[...]
    hot = (
        (lax.broadcasted_iota(jnp.int32, (LANES, beams), 0) == (point & (LANES - 1)))
        .astype(jnp.float32)
        .astype(jnp.bfloat16)
    )
    spots = jnp.dot(stack.astype(jnp.bfloat16), hot, preferred_element_type=jnp.float32)
    group = point // LANES
    found = jnp.where(group == 0, spots[0:8], 0.0)
    for g in range(1, groups):
        found = found + jnp.where(group == g, spots[8 * g : 8 * g + 8], 0.0)
    dirs[...] = jnp.transpose(jnp.concatenate([found] * 4, 0)).astype(jnp.bfloat16)
    place = pos_ref[...] * ratio
    places = jnp.concatenate(
        [jnp.concatenate([third] * 3 + [jnp.zeros_like(third)], 0) for third in thirds(place)]
        + [jnp.zeros((8, stations), jnp.float32)],
        0,
    ).astype(jnp.bfloat16)

    outgoing = []
    incoming[3].wait()
    half = samples // 2
    row = lax.broadcasted_iota(jnp.int32, (samples, samples), 0)
    column = lax.broadcasted_iota(jnp.int32, (samples, samples), 1)
    source = jnp.where(column < half, 2 * column, 2 * (column - half) + 1)
    spread = (row == source).astype(jnp.float32).astype(jnp.bfloat16)
    for polar in range(2):
        turned = lax.dot_general(
            volts_ref[polar], spread, (((0,), (0,)), ((), ())), preferred_element_type=jnp.float32
        )
        rhs_ref[polar] = turned.astype(jnp.bfloat16)
        outgoing.append(start(rhs_ref.at[polar], rhs_hbm.at[polar], out_sems.at[blocks + polar]))
    sine_c, cosine_c = fit_polynomials()
    magic = 12582912.0
    per_block = beams // blocks
    for block in range(blocks):
        for step in range(per_block // rows):
            at = pl.ds(block * per_block + step * rows, rows)
            turns = jnp.dot(dirs[at, :], places, preferred_element_type=jnp.float32)
            x = turns - ((turns + magic) - magic)
            square = x * x
            s = x * horner(sine_c, square)
            c = horner(cosine_c, square)
            phase_ref[0, at, :] = 1.0 - s * s
            phase_ref[1, at, :] = s * c
        part = pl.ds(block * per_block, per_block)
        outgoing.append(start(phase_ref.at[:, part], phase_hbm.at[:, part], out_sems.at[block]))

    for copy in outgoing:
        copy.wait()


def phasors(volts, positions, directions, pointing, total):
    beams = pointing.shape[1]
    stations = positions.shape[1]
    samples = volts.shape[1]
    blocks = 8
    phase = (2, beams, stations)
    rhs = (2, 2 * stations, samples)
    return pl.pallas_call(
        functools.partial(phasor_kernel, 64, blocks, total),
        out_shape=(
            jax.ShapeDtypeStruct(phase, jnp.float32),
            jax.ShapeDtypeStruct(rhs, jnp.bfloat16),
        ),
        in_specs=[HBM_SPEC] * 4,
        out_specs=(HBM_SPEC, HBM_SPEC),
        scratch_shapes=[
            pltpu.VMEM(volts.shape, volts.dtype),
            pltpu.VMEM(positions.shape, jnp.float32),
            pltpu.VMEM(directions.shape, jnp.float32),
            pltpu.VMEM(pointing.shape, jnp.int32),
            pltpu.VMEM(phase, jnp.float32),
            pltpu.VMEM(rhs, jnp.bfloat16),
            pltpu.VMEM((beams, 32), jnp.bfloat16),
            pltpu.SemaphoreType.DMA((4,)),
            pltpu.SemaphoreType.DMA((blocks + 2,)),
        ],
        compiler_params=pltpu.CompilerParams(vmem_limit_bytes=GRANT - 2 * MIB),
        cost_estimate=pl.CostEstimate(
            flops=60 * beams * stations, bytes_accessed=8 * MIB, transcendentals=0
        ),
        name="phasors",
    )(volts, positions, directions, pointing)


def invert_small(left):
    order = len(left)
    unit = jnp.ones_like(left[0][0])
    nothing = jnp.zeros_like(unit)
    right = [[unit if r == c else nothing for c in range(order)] for r in range(order)]
    for pivot in range(order):
        factor = 1.0 / left[pivot][pivot]
        left[pivot] = [entry * factor for entry in left[pivot]]
        right[pivot] = [entry * factor for entry in right[pivot]]
        for r in range(order):
            if r != pivot:
                scale = left[r][pivot]
                left[r] = [a - scale * b for a, b in zip(left[r], left[pivot])]
                right[r] = [a - scale * b for a, b in zip(right[r], right[pivot])]
    return right


def combine(weights, values):
    total = None
    for w, v in zip(weights, values):
        term = v if isinstance(w, float) and w == 1.0 else w * v
        total = term if total is None else total + term
    return total


def solve(cal_ref, target, keep, lean, history):
    total = cal_ref.shape[0]
    half = cal_ref.shape[2]
    table = basis_table(total)
    pairs = [(c, total - 1 - c, [float(v) for v in table[c]]) for c in range(total // 2)]

    def gather_sums(sums, first, second, line):
        even, odd = first + second, first - second
        terms = (even, line[1] * odd, line[2] * even, line[3] * odd)
        return [t if s is None else s + t for s, t in zip(sums, terms)]

    gram = [[None] * ORDER for _ in range(ORDER)]
    sums = [None] * ORDER
    for first, second, line in pairs:
        masks, values = [], []
        for c in (first, second):
            block = cal_ref[c].astype(jnp.float32)
            weight = block[8:16]
            mask = jnp.where(weight > 0.0, 1.0, 0.0)
            inverse = 1.0 / (weight + PENALTY)
            gain = mask * (PENALTY * inverse)
            value = block[0:8] * inverse
            target[c] = value
            history[c] = value
            keep[c] = mask - gain
            lean[c] = 2.0 * gain - mask
            masks.append(mask)
            values.append(value)
        sums = gather_sums(sums, *values, line)
        even, odd = masks[0] + masks[1], masks[0] - masks[1]
        for k in range(ORDER):
            for j in range(k, ORDER):
                term = (even if (k + j) % 2 == 0 else odd) * (line[k] * line[j])
                gram[k][j] = term if gram[k][j] is None else gram[k][j] + term
    for k in range(ORDER):
        gram[k][k] = gram[k][k] + RIDGE
        for j in range(k):
            gram[k][j] = gram[j][k]
    inverse = invert_small(gram)
    coefficients = tuple(combine(inverse[k], sums) for k in range(ORDER))

    def sweep(_, coefficients):
        sums = [None] * ORDER
        for first, second, line in pairs:
            even = coefficients[0] + line[2] * coefficients[2]
            odd = line[1] * coefficients[1] + line[3] * coefficients[3]
            values = []
            for c, fitted in ((first, even + odd), (second, even - odd)):
                u = (target[c] + keep[c] * history[c]) + lean[c] * fitted
                history[c] = u
                values.append(u)
            sums = gather_sums(sums, *values, line)
        return tuple(combine(inverse[k], sums) for k in range(ORDER))

    coefficients = lax.fori_loop(1, ITERS, sweep, coefficients)
    channel = lax.axis_index("chan").astype(jnp.float32)
    place = 2.0 * (channel + 0.5) / total - 1.0
    return combine(legendre(place), coefficients)


def beam_kernel(
    blocks, cal_hbm, phase_hbm, rhs_hbm, out_ref, fitted_ref,
    cal_ref, phase_ref, rhs_ref, target, keep, lean, history, sems,
):
    stations = phase_ref.shape[2]
    half = rhs_ref.shape[2] // 2
    per_block = phase_ref.shape[1] // blocks
    cal_copy = start(cal_hbm, cal_ref, sems.at[0])
    rhs_copy = start(rhs_hbm, rhs_ref, sems.at[1])

    def fetch(block):
        part = pl.ds(block * per_block, per_block)
        return start(phase_hbm.at[:, part], phase_ref.at[:, part], sems.at[2 + block])

    copies = [fetch(0)]
    cal_copy.wait()
    fitted = solve(cal_ref, target, keep, lean, history)
    fitted_ref[:, : stations // 2] = fitted[0:4]
    fitted_ref[:, stations // 2 :] = fitted[4:8]
    own = cal_ref[lax.axis_index("chan")].astype(jnp.float32)[8:16]
    dense = fitted * jnp.where(own > 0.0, stations ** (-0.5), 0.0)
    gains = jnp.concatenate([dense[0:4], dense[4:8]], 1)
    rhs_copy.wait()
    for block in range(blocks):
        part = pl.ds(block * per_block, per_block)
        copies[block].wait()
        if block == 0:
            copies += [fetch(later) for later in range(1, blocks)]
        cosine = phase_ref[0, part]
        sine = phase_ref[1, part]
        power = None
        for polar in range(2):
            re = gains[2 * polar : 2 * polar + 1]
            im = gains[2 * polar + 1 : 2 * polar + 2]
            w_re = (re * cosine - im * sine).astype(jnp.bfloat16)
            w_im = (-(re * sine + im * cosine)).astype(jnp.bfloat16)
            lhs = jnp.concatenate(
                [jnp.concatenate([w_re, -w_im], 1), jnp.concatenate([w_im, w_re], 1)], 0
            )
            y = jnp.dot(lhs, rhs_ref[polar], preferred_element_type=jnp.float32)
            y = y * y
            y = y[:per_block] + y[per_block:]
            power = y if power is None else power + y
        out_ref[part, :] = ((power[:, :half] + power[:, half:]) * 0.5).astype(jnp.bfloat16)


def fit_and_detect(cal, phase, rhs):
    total, _, half_stations = cal.shape
    _, beams, stations = phase.shape
    samples = rhs.shape[2]
    blocks = 2
    state = pltpu.VMEM((total, 8, half_stations), jnp.float32)
    return pl.pallas_call(
        functools.partial(beam_kernel, blocks),
        out_shape=(
            jax.ShapeDtypeStruct((beams, samples // 2), jnp.bfloat16),
            jax.ShapeDtypeStruct((4, stations), jnp.float32),
        ),
        in_specs=[HBM_SPEC] * 3,
        out_specs=(VMEM_SPEC, VMEM_SPEC),
        scratch_shapes=[
            pltpu.VMEM(cal.shape, cal.dtype),
            pltpu.VMEM(phase.shape, jnp.float32),
            pltpu.VMEM(rhs.shape, jnp.bfloat16),
        ]
        + [state] * 4
        + [pltpu.SemaphoreType.DMA((2 + blocks,))],
        compiler_params=pltpu.CompilerParams(vmem_limit_bytes=GRANT - 11 * MIB),
        name="beams",
    )(cal, phase, rhs)


def body(voltages, cal_num, cal_weight, flags, positions, directions, pointing):
    devices = lax.axis_size("chan")
    assert voltages.shape[0] == 1
    total = devices
    packed = pack(cal_num[0], cal_weight[0], flags, devices)
    cal = lax.all_to_all(packed, "chan", 0, 0, tiled=True)
    phase, rhs = phasors(voltages[0], positions, directions, pointing[None, :], total)
    power, fitted = fit_and_detect(cal, phase, rhs)
    moved = lax.all_to_all(power, "chan", 0, 0, tiled=True)
    beams = power.shape[0] // devices
    beam_power = jnp.transpose(moved.reshape(devices, beams, power.shape[1]), (1, 0, 2))
    return beam_power, fitted[None]


def solution(mesh):
    return jax.shard_map(
        body,
        mesh=mesh,
        in_specs=(
            P(("group", "chan"), None, None, None),
            P(("group", "chan"), None, None),
            P(("group", "chan"), None, None),
            P(("group", "chan"), None),
            P(),
            P(),
            P("group"),
        ),
        out_specs=(P(("group", "chan"), None, None), P(("group", "chan"), None, None)),
        check_vma=False,
    )
```

```python
import functools

import jax
import jax.numpy as jnp
import numpy as np
from jax import lax
from jax.experimental import pallas as pl
from jax.experimental.pallas import tpu as pltpu
from jax.sharding import PartitionSpec as P

ITERS = 8
ORDER = 4
PENALTY = 2.0
RIDGE = 1.0
MIB = 1 << 20
LANES = 128
GRANT = 67_000_000


def legendre(place):
    return [
        1.0,
        place,
        0.5 * (3.0 * place * place - 1.0),
        0.5 * (5.0 * place * place * place - 3.0 * place),
    ]


def basis_table(total):
    place = np.float32(2.0) * (np.arange(total, dtype=np.float32) + np.float32(0.5)) / np.float32(
        total
    ) - np.float32(1.0)
    return np.stack([np.broadcast_to(np.float32(v), place.shape) for v in legendre(place)], 1)


HBM_SPEC = pl.BlockSpec(memory_space=pltpu.HBM)
VMEM_SPEC = pl.BlockSpec(memory_space=pltpu.VMEM)


def start(source, target, semaphore):
    copy = pltpu.make_async_copy(source, target, semaphore)
    copy.start()
    return copy


NUM_MOST = 6.0
WEIGHT_MOST = 5.0
LEVELS = 32767.0
STEPS = 14


def stacked(x):
    half = x.shape[1] // 2
    return jnp.concatenate([x[:, :half], x[:, half:]], 0)


def even_rows(x):
    return lax.broadcasted_iota(jnp.int32, x.shape, 0) % 2 == 0


def beside(x, even):
    return jnp.where(even, pltpu.roll(x, 7, 0), pltpu.roll(x, 1, 0))


def pack_kernel(num_hbm, weight_hbm, flag_hbm, out_ref, num_ref, weight_ref, flag_ref, sems):
    copies = [
        start(num_hbm, num_ref, sems.at[0]),
        start(weight_hbm, weight_ref, sems.at[1]),
        start(flag_hbm, flag_ref, sems.at[2]),
    ]
    for copy in copies:
        copy.wait()
    mask = flag_ref[...].astype(jnp.float32)
    num = stacked(num_ref[...] * mask)
    weight = weight_ref[...] * mask
    weight = stacked(jnp.concatenate([weight[0:1], weight[0:1], weight[1:2], weight[1:2]], 0))
    even = even_rows(num)
    size = jnp.abs(num)
    size = jnp.maximum(size, beside(size, even))
    scale = jnp.ones_like(size)
    inverse = jnp.ones_like(size)
    for power in range(1, STEPS + 1):
        larger = size > NUM_MOST * 2.0 ** (power - 1 - STEPS)
        scale = jnp.where(larger, 2.0**power, scale)
        inverse = jnp.where(larger, 2.0**-power, inverse)
    coded = jnp.round(num * inverse * (LEVELS * 2.0**STEPS / NUM_MOST))
    coded = jnp.clip(coded, -LEVELS, LEVELS)
    level = jnp.clip(jnp.round(weight * (LEVELS / WEIGHT_MOST)), 0.0, LEVELS)
    block = jnp.concatenate([coded, jnp.where(even, level, scale)], 0)
    block = block.astype(jnp.int32).astype(out_ref.dtype)
    for peer in range(out_ref.shape[0]):
        out_ref[peer] = block


def unpack(block):
    block = block.astype(jnp.int32).astype(jnp.float32)
    coded, side = block[0:8], block[8:16]
    even = even_rows(side)
    weight = jnp.where(even, side, pltpu.roll(side, 1, 0)) * (WEIGHT_MOST / LEVELS)
    scale = jnp.where(even, pltpu.roll(side, 7, 0), side)
    return coded * (scale * (NUM_MOST / (LEVELS * 2.0**STEPS))), weight


def pack(cal_num, cal_weight, flags, devices):
    stations = cal_num.shape[1]
    return pl.pallas_call(
        pack_kernel,
        out_shape=jax.ShapeDtypeStruct((devices, 16, stations // 2), jnp.int16),
        in_specs=[HBM_SPEC] * 3,
        out_specs=VMEM_SPEC,
        scratch_shapes=[
            pltpu.VMEM(cal_num.shape, jnp.float32),
            pltpu.VMEM(cal_weight.shape, jnp.float32),
            pltpu.VMEM(flags.shape, jnp.int32),
            pltpu.SemaphoreType.DMA((3,)),
        ],
        compiler_params=pltpu.CompilerParams(vmem_limit_bytes=GRANT),
        name="pack",
    )(cal_num, cal_weight, flags)


def fit_polynomials():
    nodes = np.cos(np.pi * (np.arange(400) + 0.5) / 400) * 0.5
    square = nodes * nodes
    safe = np.sinc(nodes) * np.pi
    chebyshev = np.polynomial.chebyshev.Chebyshev
    sine = chebyshev.fit(square, safe, 4, domain=[0, 0.25])
    cosine = chebyshev.fit(square, np.cos(np.pi * nodes), 5, domain=[0, 0.25])
    to_power = lambda c: c.convert(kind=np.polynomial.Polynomial).coef * np.sqrt(2.0)
    return [float(np.float32(v)) for v in to_power(sine)], [
        float(np.float32(v)) for v in to_power(cosine)
    ]


def horner(coefficients, x):
    value = coefficients[-1]
    for c in coefficients[-2::-1]:
        value = value * x + c
    return value


def thirds(x):
    high = x.astype(jnp.bfloat16).astype(jnp.float32)
    middle = (x - high).astype(jnp.bfloat16).astype(jnp.float32)
    return [high, middle, x - high - middle]


def phasor_kernel(
    rows, blocks, total, volts_hbm, pos_hbm, dir_hbm, point_hbm, phase_hbm, rhs_hbm,
    volts_ref, pos_ref, dir_ref, point_ref, phase_ref, rhs_ref, dirs, sems, out_sems,
):
    incoming = [
        start(point_hbm, point_ref, sems.at[0]),
        start(dir_hbm, dir_ref, sems.at[1]),
        start(pos_hbm, pos_ref, sems.at[2]),
        start(volts_hbm, volts_ref, sems.at[3]),
    ]
    table = dir_ref.shape[1]
    beams = point_ref.shape[1]
    stations = pos_ref.shape[1]
    samples = volts_ref.shape[1]
    channel = lax.axis_index("chan").astype(jnp.float32)
    ratio = 1.0 + 0.3 * (channel + 0.5) / total
    for copy in incoming[:3]:
        copy.wait()

    parts = jnp.concatenate(thirds(dir_ref[...]) + [jnp.zeros_like(dir_ref[...])], 0)
    groups = table // LANES
    stack = jnp.concatenate([parts[:, g * LANES : (g + 1) * LANES] for g in range(groups)], 0)
    point = point_ref[...]
    hot = (
        (lax.broadcasted_iota(jnp.int32, (LANES, beams), 0) == (point & (LANES - 1)))
        .astype(jnp.float32)
        .astype(jnp.bfloat16)
    )
    spots = jnp.dot(stack.astype(jnp.bfloat16), hot, preferred_element_type=jnp.float32)
    group = point // LANES
    found = jnp.where(group == 0, spots[0:8], 0.0)
    for g in range(1, groups):
        found = found + jnp.where(group == g, spots[8 * g : 8 * g + 8], 0.0)
    dirs[...] = jnp.transpose(jnp.concatenate([found] * 4, 0)).astype(jnp.bfloat16)
    place = pos_ref[...] * ratio
    places = jnp.concatenate(
        [jnp.concatenate([third] * 3 + [jnp.zeros_like(third)], 0) for third in thirds(place)]
        + [jnp.zeros((8, stations), jnp.float32)],
        0,
    ).astype(jnp.bfloat16)

    outgoing = []
    incoming[3].wait()
    half = samples // 2
    row = lax.broadcasted_iota(jnp.int32, (samples, samples), 0)
    column = lax.broadcasted_iota(jnp.int32, (samples, samples), 1)
    source = jnp.where(column < half, 2 * column, 2 * (column - half) + 1)
    spread = (row == source).astype(jnp.float32).astype(jnp.bfloat16)
    for polar in range(2):
        turned = lax.dot_general(
            volts_ref[polar], spread, (((0,), (0,)), ((), ())), preferred_element_type=jnp.float32
        )
        rhs_ref[polar] = turned.astype(jnp.bfloat16)
        outgoing.append(start(rhs_ref.at[polar], rhs_hbm.at[polar], out_sems.at[blocks + polar]))
    sine_c, cosine_c = fit_polynomials()
    magic = 12582912.0
    per_block = beams // blocks
    for block in range(blocks):
        for step in range(per_block // rows):
            at = pl.ds(block * per_block + step * rows, rows)
            turns = jnp.dot(dirs[at, :], places, preferred_element_type=jnp.float32)
            x = turns - ((turns + magic) - magic)
            square = x * x
            s = x * horner(sine_c, square)
            c = horner(cosine_c, square)
            phase_ref[0, at, :] = 1.0 - s * s
            phase_ref[1, at, :] = s * c
        part = pl.ds(block * per_block, per_block)
        outgoing.append(start(phase_ref.at[:, part], phase_hbm.at[:, part], out_sems.at[block]))

    for copy in outgoing:
        copy.wait()


def phasors(volts, positions, directions, pointing, total):
    beams = pointing.shape[1]
    stations = positions.shape[1]
    samples = volts.shape[1]
    blocks = 8
    phase = (2, beams, stations)
    rhs = (2, 2 * stations, samples)
    return pl.pallas_call(
        functools.partial(phasor_kernel, 64, blocks, total),
        out_shape=(
            jax.ShapeDtypeStruct(phase, jnp.float32),
            jax.ShapeDtypeStruct(rhs, jnp.bfloat16),
        ),
        in_specs=[HBM_SPEC] * 4,
        out_specs=(HBM_SPEC, HBM_SPEC),
        scratch_shapes=[
            pltpu.VMEM(volts.shape, volts.dtype),
            pltpu.VMEM(positions.shape, jnp.float32),
            pltpu.VMEM(directions.shape, jnp.float32),
            pltpu.VMEM(pointing.shape, jnp.int32),
            pltpu.VMEM(phase, jnp.float32),
            pltpu.VMEM(rhs, jnp.bfloat16),
            pltpu.VMEM((beams, 32), jnp.bfloat16),
            pltpu.SemaphoreType.DMA((4,)),
            pltpu.SemaphoreType.DMA((blocks + 2,)),
        ],
        compiler_params=pltpu.CompilerParams(vmem_limit_bytes=GRANT - 2 * MIB),
        cost_estimate=pl.CostEstimate(
            flops=60 * beams * stations, bytes_accessed=8 * MIB, transcendentals=0
        ),
        name="phasors",
    )(volts, positions, directions, pointing)


def invert_small(left):
    order = len(left)
    unit = jnp.ones_like(left[0][0])
    nothing = jnp.zeros_like(unit)
    right = [[unit if r == c else nothing for c in range(order)] for r in range(order)]
    for pivot in range(order):
        factor = 1.0 / left[pivot][pivot]
        left[pivot] = [entry * factor for entry in left[pivot]]
        right[pivot] = [entry * factor for entry in right[pivot]]
        for r in range(order):
            if r != pivot:
                scale = left[r][pivot]
                left[r] = [a - scale * b for a, b in zip(left[r], left[pivot])]
                right[r] = [a - scale * b for a, b in zip(right[r], right[pivot])]
    return right


def combine(weights, values):
    total = None
    for w, v in zip(weights, values):
        term = v if isinstance(w, float) and w == 1.0 else w * v
        total = term if total is None else total + term
    return total


def solve(cal_ref, target, keep, lean, history):
    total = cal_ref.shape[0]
    half = cal_ref.shape[2]
    table = basis_table(total)
    pairs = [(c, total - 1 - c, [float(v) for v in table[c]]) for c in range(total // 2)]

    def gather_sums(sums, first, second, line):
        even, odd = first + second, first - second
        terms = (even, line[1] * odd, line[2] * even, line[3] * odd)
        return [t if s is None else s + t for s, t in zip(sums, terms)]

    gram = [[None] * ORDER for _ in range(ORDER)]
    sums = [None] * ORDER
    for first, second, line in pairs:
        masks, values = [], []
        for c in (first, second):
            num, weight = unpack(cal_ref[c])
            mask = jnp.where(weight > 0.0, 1.0, 0.0)
            inverse = 1.0 / (weight + PENALTY)
            gain = mask * (PENALTY * inverse)
            value = num * inverse
            target[c] = value
            history[c] = value
            keep[c] = mask - gain
            lean[c] = 2.0 * gain - mask
            masks.append(mask)
            values.append(value)
        sums = gather_sums(sums, *values, line)
        even, odd = masks[0] + masks[1], masks[0] - masks[1]
        for k in range(ORDER):
            for j in range(k, ORDER):
                term = (even if (k + j) % 2 == 0 else odd) * (line[k] * line[j])
                gram[k][j] = term if gram[k][j] is None else gram[k][j] + term
    for k in range(ORDER):
        gram[k][k] = gram[k][k] + RIDGE
        for j in range(k):
            gram[k][j] = gram[j][k]
    inverse = invert_small(gram)
    coefficients = tuple(combine(inverse[k], sums) for k in range(ORDER))

    def sweep(_, coefficients):
        sums = [None] * ORDER
        for first, second, line in pairs:
            even = coefficients[0] + line[2] * coefficients[2]
            odd = line[1] * coefficients[1] + line[3] * coefficients[3]
            values = []
            for c, fitted in ((first, even + odd), (second, even - odd)):
                u = (target[c] + keep[c] * history[c]) + lean[c] * fitted
                history[c] = u
                values.append(u)
            sums = gather_sums(sums, *values, line)
        return tuple(combine(inverse[k], sums) for k in range(ORDER))

    coefficients = lax.fori_loop(1, ITERS, sweep, coefficients)
    channel = lax.axis_index("chan").astype(jnp.float32)
    place = 2.0 * (channel + 0.5) / total - 1.0
    return combine(legendre(place), coefficients)


def beam_kernel(
    blocks, cal_hbm, phase_hbm, rhs_hbm, out_ref, fitted_ref,
    cal_ref, phase_ref, rhs_ref, target, keep, lean, history, sems,
):
    stations = phase_ref.shape[2]
    half = rhs_ref.shape[2] // 2
    per_block = phase_ref.shape[1] // blocks
    cal_copy = start(cal_hbm, cal_ref, sems.at[0])
    rhs_copy = start(rhs_hbm, rhs_ref, sems.at[1])

    def fetch(block):
        part = pl.ds(block * per_block, per_block)
        return start(phase_hbm.at[:, part], phase_ref.at[:, part], sems.at[2 + block])

    copies = [fetch(0)]
    cal_copy.wait()
    fitted = solve(cal_ref, target, keep, lean, history)
    fitted_ref[:, : stations // 2] = fitted[0:4]
    fitted_ref[:, stations // 2 :] = fitted[4:8]
    _, own = unpack(cal_ref[lax.axis_index("chan")])
    dense = fitted * jnp.where(own > 0.0, stations ** (-0.5), 0.0)
    gains = jnp.concatenate([dense[0:4], dense[4:8]], 1)
    rhs_copy.wait()
    for block in range(blocks):
        part = pl.ds(block * per_block, per_block)
        copies[block].wait()
        if block == 0:
            copies += [fetch(later) for later in range(1, blocks)]
        cosine = phase_ref[0, part]
        sine = phase_ref[1, part]
        power = None
        for polar in range(2):
            re = gains[2 * polar : 2 * polar + 1]
            im = gains[2 * polar + 1 : 2 * polar + 2]
            w_re = (re * cosine - im * sine).astype(jnp.bfloat16)
            w_im = (-(re * sine + im * cosine)).astype(jnp.bfloat16)
            lhs = jnp.concatenate(
                [jnp.concatenate([w_re, -w_im], 1), jnp.concatenate([w_im, w_re], 1)], 0
            )
            y = jnp.dot(lhs, rhs_ref[polar], preferred_element_type=jnp.float32)
            y = y * y
            y = y[:per_block] + y[per_block:]
            power = y if power is None else power + y
        out_ref[part, :] = ((power[:, :half] + power[:, half:]) * 0.5).astype(jnp.bfloat16)


def fit_and_detect(cal, phase, rhs):
    total, _, half_stations = cal.shape
    _, beams, stations = phase.shape
    samples = rhs.shape[2]
    blocks = 2
    state = pltpu.VMEM((total, 8, half_stations), jnp.float32)
    return pl.pallas_call(
        functools.partial(beam_kernel, blocks),
        out_shape=(
            jax.ShapeDtypeStruct((beams, samples // 2), jnp.bfloat16),
            jax.ShapeDtypeStruct((4, stations), jnp.float32),
        ),
        in_specs=[HBM_SPEC] * 3,
        out_specs=(VMEM_SPEC, VMEM_SPEC),
        scratch_shapes=[
            pltpu.VMEM(cal.shape, cal.dtype),
            pltpu.VMEM(phase.shape, jnp.float32),
            pltpu.VMEM(rhs.shape, jnp.bfloat16),
        ]
        + [state] * 4
        + [pltpu.SemaphoreType.DMA((2 + blocks,))],
        compiler_params=pltpu.CompilerParams(vmem_limit_bytes=GRANT - 11 * MIB),
        name="beams",
    )(cal, phase, rhs)


def body(voltages, cal_num, cal_weight, flags, positions, directions, pointing):
    devices = lax.axis_size("chan")
    assert voltages.shape[0] == 1
    total = devices
    packed = pack(cal_num[0], cal_weight[0], flags, devices)
    cal = lax.all_to_all(packed, "chan", 0, 0, tiled=True)
    phase, rhs = phasors(voltages[0], positions, directions, pointing[None, :], total)
    power, fitted = fit_and_detect(cal, phase, rhs)
    moved = lax.all_to_all(power, "chan", 0, 0, tiled=True)
    beams = power.shape[0] // devices
    beam_power = jnp.transpose(moved.reshape(devices, beams, power.shape[1]), (1, 0, 2))
    return beam_power, fitted[None]


def solution(mesh):
    return jax.shard_map(
        body,
        mesh=mesh,
        in_specs=(
            P(("group", "chan"), None, None, None),
            P(("group", "chan"), None, None),
            P(("group", "chan"), None, None),
            P(("group", "chan"), None),
            P(),
            P(),
            P("group"),
        ),
        out_specs=(P(("group", "chan"), None, None), P(("group", "chan"), None, None)),
        check_vma=False,
    )
```

```python
import functools

import jax
import jax.numpy as jnp
import numpy as np
from jax import lax
from jax.experimental import pallas as pl
from jax.experimental.pallas import tpu as pltpu
from jax.sharding import PartitionSpec as P

ITERS = 8
ORDER = 4
PENALTY = 2.0
RIDGE = 1.0
MIB = 1 << 20
LANES = 128
GRANT = 67_000_000


def legendre(place):
    return [
        1.0,
        place,
        0.5 * (3.0 * place * place - 1.0),
        0.5 * (5.0 * place * place * place - 3.0 * place),
    ]


def basis_table(total):
    place = np.float32(2.0) * (np.arange(total, dtype=np.float32) + np.float32(0.5)) / np.float32(
        total
    ) - np.float32(1.0)
    return np.stack([np.broadcast_to(np.float32(v), place.shape) for v in legendre(place)], 1)


HBM_SPEC = pl.BlockSpec(memory_space=pltpu.HBM)
VMEM_SPEC = pl.BlockSpec(memory_space=pltpu.VMEM)


def start(source, target, semaphore):
    copy = pltpu.make_async_copy(source, target, semaphore)
    copy.start()
    return copy


NUM_MOST = 6.0
WEIGHT_MOST = 5.0
LEVELS = 32767.0
STEPS = 14


def stacked(x):
    half = x.shape[1] // 2
    return jnp.concatenate([x[:, :half], x[:, half:]], 0)


def even_rows(x):
    return lax.broadcasted_iota(jnp.int32, x.shape, 0) % 2 == 0


def beside(x, even):
    return jnp.where(even, pltpu.roll(x, 7, 0), pltpu.roll(x, 1, 0))


def pack_kernel(num_hbm, weight_hbm, flag_hbm, out_ref, num_ref, weight_ref, flag_ref, sems):
    copies = [
        start(num_hbm, num_ref, sems.at[0]),
        start(weight_hbm, weight_ref, sems.at[1]),
        start(flag_hbm, flag_ref, sems.at[2]),
    ]
    for copy in copies:
        copy.wait()
    mask = flag_ref[...].astype(jnp.float32)
    num = stacked(num_ref[...] * mask)
    weight = weight_ref[...] * mask
    weight = stacked(jnp.concatenate([weight[0:1], weight[0:1], weight[1:2], weight[1:2]], 0))
    even = even_rows(num)
    size = jnp.abs(num)
    size = jnp.maximum(size, beside(size, even))
    scale = jnp.ones_like(size)
    inverse = jnp.ones_like(size)
    for power in range(1, STEPS + 1):
        larger = size > NUM_MOST * 2.0 ** (power - 1 - STEPS)
        scale = jnp.where(larger, 2.0**power, scale)
        inverse = jnp.where(larger, 2.0**-power, inverse)
    coded = jnp.round(num * inverse * (LEVELS * 2.0**STEPS / NUM_MOST))
    coded = jnp.clip(coded, -LEVELS, LEVELS)
    level = jnp.clip(jnp.round(weight * (LEVELS / WEIGHT_MOST)), 0.0, LEVELS)
    block = jnp.concatenate([coded, jnp.where(even, level, scale)], 0)
    block = block.astype(jnp.int32).astype(out_ref.dtype)
    for peer in range(out_ref.shape[0]):
        out_ref[peer] = block


def unpack(block):
    block = block.astype(jnp.int32).astype(jnp.float32)
    coded, side = block[0:8], block[8:16]
    even = even_rows(side)
    weight = jnp.where(even, side, pltpu.roll(side, 1, 0)) * (WEIGHT_MOST / LEVELS)
    scale = jnp.where(even, pltpu.roll(side, 7, 0), side)
    return coded * (scale * (NUM_MOST / (LEVELS * 2.0**STEPS))), weight


def pack(cal_num, cal_weight, flags, devices):
    stations = cal_num.shape[1]
    return pl.pallas_call(
        pack_kernel,
        out_shape=jax.ShapeDtypeStruct((devices, 16, stations // 2), jnp.int16),
        in_specs=[HBM_SPEC] * 3,
        out_specs=VMEM_SPEC,
        scratch_shapes=[
            pltpu.VMEM(cal_num.shape, jnp.float32),
            pltpu.VMEM(cal_weight.shape, jnp.float32),
            pltpu.VMEM(flags.shape, jnp.int32),
            pltpu.SemaphoreType.DMA((3,)),
        ],
        compiler_params=pltpu.CompilerParams(vmem_limit_bytes=GRANT),
        name="pack",
    )(cal_num, cal_weight, flags)


def fit_polynomials():
    nodes = np.cos(np.pi * (np.arange(400) + 0.5) / 400) * 0.5
    square = nodes * nodes
    safe = np.sinc(nodes) * np.pi
    chebyshev = np.polynomial.chebyshev.Chebyshev
    sine = chebyshev.fit(square, safe, 4, domain=[0, 0.25])
    cosine = chebyshev.fit(square, np.cos(np.pi * nodes), 5, domain=[0, 0.25])
    to_power = lambda c: c.convert(kind=np.polynomial.Polynomial).coef * np.sqrt(2.0)
    return [float(np.float32(v)) for v in to_power(sine)], [
        float(np.float32(v)) for v in to_power(cosine)
    ]


def horner(coefficients, x):
    value = coefficients[-1]
    for c in coefficients[-2::-1]:
        value = value * x + c
    return value


def thirds(x):
    high = x.astype(jnp.bfloat16).astype(jnp.float32)
    middle = (x - high).astype(jnp.bfloat16).astype(jnp.float32)
    return [high, middle, x - high - middle]


def phasor_kernel(
    rows, blocks, total, volts_hbm, pos_hbm, dir_hbm, point_hbm, phase_hbm, rhs_hbm,
    volts_ref, pos_ref, dir_ref, point_ref, phase_ref, rhs_ref, dirs, sems, out_sems,
):
    incoming = [
        start(point_hbm, point_ref, sems.at[0]),
        start(dir_hbm, dir_ref, sems.at[1]),
        start(pos_hbm, pos_ref, sems.at[2]),
        start(volts_hbm, volts_ref, sems.at[3]),
    ]
    table = dir_ref.shape[1]
    beams = point_ref.shape[1]
    stations = pos_ref.shape[1]
    samples = volts_ref.shape[1]
    channel = lax.axis_index("chan").astype(jnp.float32)
    ratio = 1.0 + 0.3 * (channel + 0.5) / total
    for copy in incoming[:3]:
        copy.wait()

    parts = jnp.concatenate(thirds(dir_ref[...]) + [jnp.zeros_like(dir_ref[...])], 0)
    groups = table // LANES
    stack = jnp.concatenate([parts[:, g * LANES : (g + 1) * LANES] for g in range(groups)], 0)
    point = point_ref[...]
    hot = (
        (lax.broadcasted_iota(jnp.int32, (LANES, beams), 0) == (point & (LANES - 1)))
        .astype(jnp.float32)
        .astype(jnp.bfloat16)
    )
    spots = jnp.dot(stack.astype(jnp.bfloat16), hot, preferred_element_type=jnp.float32)
    group = point // LANES
    found = jnp.where(group == 0, spots[0:8], 0.0)
    for g in range(1, groups):
        found = found + jnp.where(group == g, spots[8 * g : 8 * g + 8], 0.0)
    dirs[...] = jnp.transpose(jnp.concatenate([found] * 4, 0)).astype(jnp.bfloat16)
    place = pos_ref[...] * ratio
    places = jnp.concatenate(
        [jnp.concatenate([third] * 3 + [jnp.zeros_like(third)], 0) for third in thirds(place)]
        + [jnp.zeros((8, stations), jnp.float32)],
        0,
    ).astype(jnp.bfloat16)

    outgoing = []
    incoming[3].wait()
    half = samples // 2
    row = lax.broadcasted_iota(jnp.int32, (samples, samples), 0)
    column = lax.broadcasted_iota(jnp.int32, (samples, samples), 1)
    source = jnp.where(column < half, 2 * column, 2 * (column - half) + 1)
    spread = (row == source).astype(jnp.float32).astype(jnp.bfloat16)
    for polar in range(2):
        turned = lax.dot_general(
            volts_ref[polar], spread, (((0,), (0,)), ((), ())), preferred_element_type=jnp.float32
        )
        rhs_ref[polar] = turned.astype(jnp.bfloat16)
        outgoing.append(start(rhs_ref.at[polar], rhs_hbm.at[polar], out_sems.at[blocks + polar]))
    sine_c, cosine_c = fit_polynomials()
    magic = 12582912.0
    per_block = beams // blocks
    for block in range(blocks):
        for step in range(per_block // rows):
            at = pl.ds(block * per_block + step * rows, rows)
            turns = jnp.dot(dirs[at, :], places, preferred_element_type=jnp.float32)
            x = turns - ((turns + magic) - magic)
            square = x * x
            s = x * horner(sine_c, square)
            c = horner(cosine_c, square)
            phase_ref[0, at, :] = 1.0 - s * s
            phase_ref[1, at, :] = s * c
        part = pl.ds(block * per_block, per_block)
        outgoing.append(start(phase_ref.at[:, part], phase_hbm.at[:, part], out_sems.at[block]))

    for copy in outgoing:
        copy.wait()


def phasors(volts, positions, directions, pointing, total):
    beams = pointing.shape[1]
    stations = positions.shape[1]
    samples = volts.shape[1]
    blocks = 8
    phase = (2, beams, stations)
    rhs = (2, 2 * stations, samples)
    return pl.pallas_call(
        functools.partial(phasor_kernel, 64, blocks, total),
        out_shape=(
            jax.ShapeDtypeStruct(phase, jnp.float32),
            jax.ShapeDtypeStruct(rhs, jnp.bfloat16),
        ),
        in_specs=[HBM_SPEC] * 4,
        out_specs=(HBM_SPEC, HBM_SPEC),
        scratch_shapes=[
            pltpu.VMEM(volts.shape, volts.dtype),
            pltpu.VMEM(positions.shape, jnp.float32),
            pltpu.VMEM(directions.shape, jnp.float32),
            pltpu.VMEM(pointing.shape, jnp.int32),
            pltpu.VMEM(phase, jnp.float32),
            pltpu.VMEM(rhs, jnp.bfloat16),
            pltpu.VMEM((beams, 32), jnp.bfloat16),
            pltpu.SemaphoreType.DMA((4,)),
            pltpu.SemaphoreType.DMA((blocks + 2,)),
        ],
        compiler_params=pltpu.CompilerParams(vmem_limit_bytes=GRANT - 2 * MIB),
        cost_estimate=pl.CostEstimate(
            flops=60 * beams * stations, bytes_accessed=8 * MIB, transcendentals=0
        ),
        name="phasors",
    )(volts, positions, directions, pointing)


def invert_small(left):
    order = len(left)
    unit = jnp.ones_like(left[0][0])
    nothing = jnp.zeros_like(unit)
    right = [[unit if r == c else nothing for c in range(order)] for r in range(order)]
    for pivot in range(order):
        factor = 1.0 / left[pivot][pivot]
        left[pivot] = [entry * factor for entry in left[pivot]]
        right[pivot] = [entry * factor for entry in right[pivot]]
        for r in range(order):
            if r != pivot:
                scale = left[r][pivot]
                left[r] = [a - scale * b for a, b in zip(left[r], left[pivot])]
                right[r] = [a - scale * b for a, b in zip(right[r], right[pivot])]
    return right


def combine(weights, values):
    total = None
    for w, v in zip(weights, values):
        term = v if isinstance(w, float) and w == 1.0 else w * v
        total = term if total is None else total + term
    return total


def solve(cal_ref, target, keep, lean, history):
    total = cal_ref.shape[0]
    half = cal_ref.shape[2]
    table = basis_table(total)
    pairs = [(c, total - 1 - c, [float(v) for v in table[c]]) for c in range(total // 2)]

    def gather_sums(sums, first, second, line):
        even, odd = first + second, first - second
        terms = (even, line[1] * odd, line[2] * even, line[3] * odd)
        return [t if s is None else s + t for s, t in zip(sums, terms)]

    gram = [[None] * ORDER for _ in range(ORDER)]
    sums = [None] * ORDER
    for first, second, line in pairs:
        masks, values = [], []
        for c in (first, second):
            num, weight = unpack(cal_ref[c])
            mask = jnp.where(weight > 0.0, 1.0, 0.0)
            inverse = 1.0 / (weight + PENALTY)
            gain = mask * (PENALTY * inverse)
            value = num * inverse
            target[c] = value
            history[c] = value
            keep[c] = mask - gain
            lean[c] = 2.0 * gain - mask
            masks.append(mask)
            values.append(value)
        sums = gather_sums(sums, *values, line)
        even, odd = masks[0] + masks[1], masks[0] - masks[1]
        for k in range(ORDER):
            for j in range(k, ORDER):
                term = (even if (k + j) % 2 == 0 else odd) * (line[k] * line[j])
                gram[k][j] = term if gram[k][j] is None else gram[k][j] + term
    for k in range(ORDER):
        gram[k][k] = gram[k][k] + RIDGE
        for j in range(k):
            gram[k][j] = gram[j][k]
    inverse = invert_small(gram)
    coefficients = tuple(combine(inverse[k], sums) for k in range(ORDER))

    def sweep(_, coefficients):
        sums = [None] * ORDER
        for first, second, line in pairs:
            even = coefficients[0] + line[2] * coefficients[2]
            odd = line[1] * coefficients[1] + line[3] * coefficients[3]
            values = []
            for c, fitted in ((first, even + odd), (second, even - odd)):
                u = (target[c] + keep[c] * history[c]) + lean[c] * fitted
                history[c] = u
                values.append(u)
            sums = gather_sums(sums, *values, line)
        return tuple(combine(inverse[k], sums) for k in range(ORDER))

    coefficients = lax.fori_loop(1, ITERS, sweep, coefficients)
    channel = lax.axis_index("chan").astype(jnp.float32)
    place = 2.0 * (channel + 0.5) / total - 1.0
    return combine(legendre(place), coefficients)


def beam_kernel(
    sizes, splits, cal_ref, phase_hbm, rhs_hbm, out_ref, fitted_ref,
    phase_ref, rhs_ref, target, keep, lean, history, sems,
):
    stations = phase_ref.shape[2]
    beams = phase_ref.shape[1]
    half = rhs_ref.shape[2] // 2
    edges = [sum(sizes[:block]) * beams // sum(sizes) for block in range(len(sizes) + 1)]

    def fetch(block):
        part = pl.ds(edges[block], edges[block + 1] - edges[block])
        return start(phase_hbm.at[:, part], phase_ref.at[:, part], sems.at[2 + block])

    copies = [fetch(0)]
    rhs_copies = [start(rhs_hbm.at[p], rhs_ref.at[p], sems.at[p]) for p in range(2)]
    copies += [fetch(later) for later in range(1, min(2, len(sizes)))]
    fitted = solve(cal_ref, target, keep, lean, history)
    fitted_ref[:, : stations // 2] = fitted[0:4]
    fitted_ref[:, stations // 2 :] = fitted[4:8]
    _, own = unpack(cal_ref[lax.axis_index("chan")])
    dense = fitted * jnp.where(own > 0.0, stations ** (-0.5), 0.0)
    gains = jnp.concatenate([dense[0:4], dense[4:8]], 1)
    for copy in rhs_copies:
        copy.wait()
    for group in range(len(sizes)):
        copies[group].wait()
        if group == 0:
            copies += [fetch(later) for later in range(2, len(sizes))]
        rows = (edges[group + 1] - edges[group]) // splits[group]
        for block in range(splits[group]):
            part = pl.ds(edges[group] + block * rows, rows)
            cosine = phase_ref[0, part]
            sine = phase_ref[1, part]
            power = None
            for polar in range(2):
                re = gains[2 * polar : 2 * polar + 1]
                im = gains[2 * polar + 1 : 2 * polar + 2]
                w_re = (re * cosine - im * sine).astype(jnp.bfloat16)
                w_im = (-(re * sine + im * cosine)).astype(jnp.bfloat16)
                lhs = jnp.concatenate(
                    [jnp.concatenate([w_re, -w_im], 1), jnp.concatenate([w_im, w_re], 1)], 0
                )
                y = jnp.dot(lhs, rhs_ref[polar], preferred_element_type=jnp.float32)
                y = y * y
                y = y[:rows] + y[rows:]
                power = y if power is None else power + y
            out_ref[part, :] = ((power[:, :half] + power[:, half:]) * 0.5).astype(jnp.bfloat16)


def fit_and_detect(cal, phase, rhs):
    total, _, half_stations = cal.shape
    _, beams, stations = phase.shape
    samples = rhs.shape[2]
    sizes, splits = (1, 3, 4), (1, 1, 1)
    state = pltpu.VMEM((total, 8, half_stations), jnp.float32)
    return pl.pallas_call(
        functools.partial(beam_kernel, sizes, splits),
        out_shape=(
            jax.ShapeDtypeStruct((beams, samples // 2), jnp.bfloat16),
            jax.ShapeDtypeStruct((4, stations), jnp.float32),
        ),
        in_specs=[VMEM_SPEC, HBM_SPEC, HBM_SPEC],
        out_specs=(VMEM_SPEC, VMEM_SPEC),
        scratch_shapes=[
            pltpu.VMEM(phase.shape, jnp.float32),
            pltpu.VMEM(rhs.shape, jnp.bfloat16),
        ]
        + [state] * 4
        + [pltpu.SemaphoreType.DMA((2 + len(sizes),))],
        compiler_params=pltpu.CompilerParams(vmem_limit_bytes=GRANT - 11 * MIB),
        name="beams",
    )(cal, phase, rhs)


def body(voltages, cal_num, cal_weight, flags, positions, directions, pointing):
    devices = lax.axis_size("chan")
    assert voltages.shape[0] == 1
    total = devices
    packed = pack(cal_num[0], cal_weight[0], flags, devices)
    cal = lax.all_to_all(packed, "chan", 0, 0, tiled=True)
    phase, rhs = phasors(voltages[0], positions, directions, pointing[None, :], total)
    power, fitted = fit_and_detect(cal, phase, rhs)
    moved = lax.all_to_all(power, "chan", 0, 0, tiled=True)
    beams = power.shape[0] // devices
    beam_power = jnp.transpose(moved.reshape(devices, beams, power.shape[1]), (1, 0, 2))
    return beam_power, fitted[None]


def solution(mesh):
    return jax.shard_map(
        body,
        mesh=mesh,
        in_specs=(
            P(("group", "chan"), None, None, None),
            P(("group", "chan"), None, None),
            P(("group", "chan"), None, None),
            P(("group", "chan"), None),
            P(),
            P(),
            P("group"),
        ),
        out_specs=(P(("group", "chan"), None, None), P(("group", "chan"), None, None)),
        check_vma=False,
    )
```

```python
import functools

import jax
import jax.numpy as jnp
import numpy as np
from jax import lax
from jax.experimental import pallas as pl
from jax.experimental.pallas import tpu as pltpu
from jax.sharding import PartitionSpec as P

ITERS = 8
ORDER = 4
PENALTY = 2.0
RIDGE = 1.0
MIB = 1 << 20
LANES = 128
NEAR = 4
SPLITS = 1
GRANT = 67_000_000


def legendre(place):
    return [
        1.0,
        place,
        0.5 * (3.0 * place * place - 1.0),
        0.5 * (5.0 * place * place * place - 3.0 * place),
    ]


def basis_table(total):
    place = np.float32(2.0) * (np.arange(total, dtype=np.float32) + np.float32(0.5)) / np.float32(
        total
    ) - np.float32(1.0)
    return np.stack([np.broadcast_to(np.float32(v), place.shape) for v in legendre(place)], 1)


HBM_SPEC = pl.BlockSpec(memory_space=pltpu.HBM)
VMEM_SPEC = pl.BlockSpec(memory_space=pltpu.VMEM)


def in_hbm(x):
    return pltpu.with_memory_space_constraint(x, pltpu.HBM)


def start(source, target, semaphore):
    copy = pltpu.make_async_copy(source, target, semaphore)
    copy.start()
    return copy


NUM_MOST = 6.0
WEIGHT_MOST = 5.0
LEVELS = 32767.0
STEPS = 14


def stacked(x):
    half = x.shape[1] // 2
    return jnp.concatenate([x[:, :half], x[:, half:]], 0)


def even_rows(x):
    return lax.broadcasted_iota(jnp.int32, x.shape, 0) % 2 == 0


def beside(x, even):
    return jnp.where(even, pltpu.roll(x, 7, 0), pltpu.roll(x, 1, 0))


def pack_kernel(num_hbm, weight_hbm, flag_hbm, out_ref, num_ref, weight_ref, flag_ref, sems):
    copies = [
        start(num_hbm, num_ref, sems.at[0]),
        start(weight_hbm, weight_ref, sems.at[1]),
        start(flag_hbm, flag_ref, sems.at[2]),
    ]
    for copy in copies:
        copy.wait()
    mask = flag_ref[...].astype(jnp.float32)
    num = stacked(num_ref[...] * mask)
    weight = weight_ref[...] * mask
    weight = stacked(jnp.concatenate([weight[0:1], weight[0:1], weight[1:2], weight[1:2]], 0))
    even = even_rows(num)
    size = jnp.abs(num)
    size = jnp.maximum(size, beside(size, even))
    scale = jnp.ones_like(size)
    inverse = jnp.ones_like(size)
    for power in range(1, STEPS + 1):
        larger = size > NUM_MOST * 2.0 ** (power - 1 - STEPS)
        scale = jnp.where(larger, 2.0**power, scale)
        inverse = jnp.where(larger, 2.0**-power, inverse)
    coded = jnp.round(num * inverse * (LEVELS * 2.0**STEPS / NUM_MOST))
    coded = jnp.clip(coded, -LEVELS, LEVELS)
    level = jnp.clip(jnp.round(weight * (LEVELS / WEIGHT_MOST)), 0.0, LEVELS)
    block = jnp.concatenate([coded, jnp.where(even, level, scale)], 0)
    block = block.astype(jnp.int32).astype(out_ref.dtype)
    for peer in range(out_ref.shape[0]):
        out_ref[peer] = block


def unpack(block):
    block = block.astype(jnp.int32).astype(jnp.float32)
    coded, side = block[0:8], block[8:16]
    even = even_rows(side)
    weight = jnp.where(even, side, pltpu.roll(side, 1, 0)) * (WEIGHT_MOST / LEVELS)
    scale = jnp.where(even, pltpu.roll(side, 7, 0), side)
    return coded * (scale * (NUM_MOST / (LEVELS * 2.0**STEPS))), weight


def pack(cal_num, cal_weight, flags, devices):
    stations = cal_num.shape[1]
    return pl.pallas_call(
        pack_kernel,
        out_shape=jax.ShapeDtypeStruct((devices, 16, stations // 2), jnp.int16),
        in_specs=[HBM_SPEC] * 3,
        out_specs=VMEM_SPEC,
        scratch_shapes=[
            pltpu.VMEM(cal_num.shape, jnp.float32),
            pltpu.VMEM(cal_weight.shape, jnp.float32),
            pltpu.VMEM(flags.shape, jnp.int32),
            pltpu.SemaphoreType.DMA((3,)),
        ],
        compiler_params=pltpu.CompilerParams(vmem_limit_bytes=GRANT),
        name="pack",
    )(cal_num, cal_weight, flags)


def fit_polynomials():
    nodes = np.cos(np.pi * (np.arange(400) + 0.5) / 400) * 0.5
    square = nodes * nodes
    safe = np.sinc(nodes) * np.pi
    chebyshev = np.polynomial.chebyshev.Chebyshev
    sine = chebyshev.fit(square, safe, 4, domain=[0, 0.25])
    cosine = chebyshev.fit(square, np.cos(np.pi * nodes), 5, domain=[0, 0.25])
    to_power = lambda c: c.convert(kind=np.polynomial.Polynomial).coef * np.sqrt(2.0)
    return [float(np.float32(v)) for v in to_power(sine)], [
        float(np.float32(v)) for v in to_power(cosine)
    ]


def horner(coefficients, x):
    value = coefficients[-1]
    for c in coefficients[-2::-1]:
        value = value * x + c
    return value


def thirds(x):
    high = x.astype(jnp.bfloat16).astype(jnp.float32)
    middle = (x - high).astype(jnp.bfloat16).astype(jnp.float32)
    return [high, middle, x - high - middle]


def phasor_kernel(
    rows, blocks, total, volts_hbm, pos_hbm, dir_hbm, point_hbm, near_ref, far_hbm, rhs_ref,
    volts_ref, pos_ref, dir_ref, point_ref, far_ref, dirs, sems, out_sems,
):
    incoming = [
        start(point_hbm, point_ref, sems.at[0]),
        start(dir_hbm, dir_ref, sems.at[1]),
        start(pos_hbm, pos_ref, sems.at[2]),
        start(volts_hbm, volts_ref, sems.at[3]),
    ]
    table = dir_ref.shape[1]
    beams = point_ref.shape[1]
    stations = pos_ref.shape[1]
    samples = volts_ref.shape[1]
    channel = lax.axis_index("chan").astype(jnp.float32)
    ratio = 1.0 + 0.3 * (channel + 0.5) / total
    for copy in incoming[:3]:
        copy.wait()

    parts = jnp.concatenate(thirds(dir_ref[...]) + [jnp.zeros_like(dir_ref[...])], 0)
    groups = table // LANES
    stack = jnp.concatenate([parts[:, g * LANES : (g + 1) * LANES] for g in range(groups)], 0)
    point = point_ref[...]
    hot = (
        (lax.broadcasted_iota(jnp.int32, (LANES, beams), 0) == (point & (LANES - 1)))
        .astype(jnp.float32)
        .astype(jnp.bfloat16)
    )
    spots = jnp.dot(stack.astype(jnp.bfloat16), hot, preferred_element_type=jnp.float32)
    group = point // LANES
    found = jnp.where(group == 0, spots[0:8], 0.0)
    for g in range(1, groups):
        found = found + jnp.where(group == g, spots[8 * g : 8 * g + 8], 0.0)
    dirs[...] = jnp.transpose(jnp.concatenate([found] * 4, 0)).astype(jnp.bfloat16)
    place = pos_ref[...] * ratio
    places = jnp.concatenate(
        [jnp.concatenate([third] * 3 + [jnp.zeros_like(third)], 0) for third in thirds(place)]
        + [jnp.zeros((8, stations), jnp.float32)],
        0,
    ).astype(jnp.bfloat16)

    outgoing = []
    incoming[3].wait()
    half = samples // 2
    row = lax.broadcasted_iota(jnp.int32, (samples, samples), 0)
    column = lax.broadcasted_iota(jnp.int32, (samples, samples), 1)
    source = jnp.where(column < half, 2 * column, 2 * (column - half) + 1)
    spread = (row == source).astype(jnp.float32).astype(jnp.bfloat16)
    for polar in range(2):
        turned = lax.dot_general(
            volts_ref[polar], spread, (((0,), (0,)), ((), ())), preferred_element_type=jnp.float32
        )
        rhs_ref[polar] = turned.astype(jnp.bfloat16)
    sine_c, cosine_c = fit_polynomials()
    near = near_ref.shape[1]
    per_block = (beams - near) // blocks

    def fill(target, first, origin, count):
        for step in range(count // rows):
            turns = jnp.dot(
                dirs[pl.ds(origin + first + step * rows, rows), :],
                places,
                preferred_element_type=jnp.float32,
            )
            x = turns - jnp.round(turns)
            square = x * x
            s = x * horner(sine_c, square)
            c = horner(cosine_c, square)
            at = pl.ds(first + step * rows, rows)
            target[0, at, :] = 1.0 - s * s
            target[1, at, :] = s * c

    for block in range(blocks):
        fill(far_ref, block * per_block, near, per_block)
        part = pl.ds(block * per_block, per_block)
        outgoing.append(start(far_ref.at[:, part], far_hbm.at[:, part], out_sems.at[block]))
    fill(near_ref, 0, 0, near)
    for copy in outgoing:
        copy.wait()


def phasors(volts, positions, directions, pointing, total):
    beams = pointing.shape[1]
    stations = positions.shape[1]
    samples = volts.shape[1]
    blocks = 4
    near = beams * NEAR // 8
    far = (2, beams - near, stations)
    rhs = (2, 2 * stations, samples)
    return pl.pallas_call(
        functools.partial(phasor_kernel, 64, blocks, total),
        out_shape=(
            jax.ShapeDtypeStruct((2, near, stations), jnp.float32),
            pltpu.HBM(far, jnp.float32),
            jax.ShapeDtypeStruct(rhs, jnp.bfloat16),
        ),
        in_specs=[HBM_SPEC] * 4,
        out_specs=(VMEM_SPEC, HBM_SPEC, VMEM_SPEC),
        scratch_shapes=[
            pltpu.VMEM(volts.shape, volts.dtype),
            pltpu.VMEM(positions.shape, jnp.float32),
            pltpu.VMEM(directions.shape, jnp.float32),
            pltpu.VMEM(pointing.shape, jnp.int32),
            pltpu.VMEM(far, jnp.float32),
            pltpu.VMEM((beams, 32), jnp.bfloat16),
            pltpu.SemaphoreType.DMA((4,)),
            pltpu.SemaphoreType.DMA((blocks,)),
        ],
        compiler_params=pltpu.CompilerParams(vmem_limit_bytes=GRANT - 24 * MIB),
        cost_estimate=pl.CostEstimate(
            flops=60 * beams * stations, bytes_accessed=8 * MIB, transcendentals=0
        ),
        name="phasors",
    )(*map(in_hbm, (volts, positions, directions, pointing)))


def invert_small(left):
    order = len(left)
    unit = jnp.ones_like(left[0][0])
    nothing = jnp.zeros_like(unit)
    right = [[unit if r == c else nothing for c in range(order)] for r in range(order)]
    for pivot in range(order):
        factor = 1.0 / left[pivot][pivot]
        left[pivot] = [entry * factor for entry in left[pivot]]
        right[pivot] = [entry * factor for entry in right[pivot]]
        for r in range(order):
            if r != pivot:
                scale = left[r][pivot]
                left[r] = [a - scale * b for a, b in zip(left[r], left[pivot])]
                right[r] = [a - scale * b for a, b in zip(right[r], right[pivot])]
    return right


def combine(weights, values):
    total = None
    for w, v in zip(weights, values):
        term = v if isinstance(w, float) and w == 1.0 else w * v
        total = term if total is None else total + term
    return total


def solve(cal_ref, target, keep, lean, history):
    total = cal_ref.shape[0]
    half = cal_ref.shape[2]
    table = basis_table(total)
    pairs = [(c, total - 1 - c, [float(v) for v in table[c]]) for c in range(total // 2)]

    def gather_sums(sums, first, second, line):
        even, odd = first + second, first - second
        terms = (even, line[1] * odd, line[2] * even, line[3] * odd)
        return [t if s is None else s + t for s, t in zip(sums, terms)]

    gram = [[None] * ORDER for _ in range(ORDER)]
    sums = [None] * ORDER
    for first, second, line in pairs:
        masks, values = [], []
        for c in (first, second):
            num, weight = unpack(cal_ref[c])
            mask = jnp.where(weight > 0.0, 1.0, 0.0)
            inverse = 1.0 / (weight + PENALTY)
            gain = mask * (PENALTY * inverse)
            value = num * inverse
            target[c] = value
            history[c] = value
            keep[c] = mask - gain
            lean[c] = 2.0 * gain - mask
            masks.append(mask)
            values.append(value)
        sums = gather_sums(sums, *values, line)
        even, odd = masks[0] + masks[1], masks[0] - masks[1]
        for k in range(ORDER):
            for j in range(k, ORDER):
                term = (even if (k + j) % 2 == 0 else odd) * (line[k] * line[j])
                gram[k][j] = term if gram[k][j] is None else gram[k][j] + term
    for k in range(ORDER):
        gram[k][k] = gram[k][k] + RIDGE
        for j in range(k):
            gram[k][j] = gram[j][k]
    inverse = invert_small(gram)
    coefficients = tuple(combine(inverse[k], sums) for k in range(ORDER))

    def sweep(_, coefficients):
        sums = [None] * ORDER
        for first, second, line in pairs:
            even = coefficients[0] + line[2] * coefficients[2]
            odd = line[1] * coefficients[1] + line[3] * coefficients[3]
            values = []
            for c, fitted in ((first, even + odd), (second, even - odd)):
                u = (target[c] + keep[c] * history[c]) + lean[c] * fitted
                history[c] = u
                values.append(u)
            sums = gather_sums(sums, *values, line)
        return tuple(combine(inverse[k], sums) for k in range(ORDER))

    coefficients = lax.fori_loop(1, ITERS, sweep, coefficients)
    channel = lax.axis_index("chan").astype(jnp.float32)
    place = 2.0 * (channel + 0.5) / total - 1.0
    return combine(legendre(place), coefficients)


def beam_kernel(
    cal_ref, near_ref, far_hbm, rhs_ref, out_ref, fitted_ref,
    far_ref, target, keep, lean, history, sems,
):
    near, stations = near_ref.shape[1:]
    half = rhs_ref.shape[2] // 2
    far_copy = start(far_hbm, far_ref, sems.at[0])
    fitted = solve(cal_ref, target, keep, lean, history)
    fitted_ref[:, : stations // 2] = fitted[0:4]
    fitted_ref[:, stations // 2 :] = fitted[4:8]
    _, own = unpack(cal_ref[lax.axis_index("chan")])
    dense = fitted * jnp.where(own > 0.0, stations ** (-0.5), 0.0)
    gains = jnp.concatenate([dense[0:4], dense[4:8]], 1)

    def detect(phase_ref, origin, splits):
        rows = phase_ref.shape[1] // splits
        for block in range(splits):
            part = pl.ds(block * rows, rows)
            cosine = phase_ref[0, part]
            sine = phase_ref[1, part]
            power = None
            for polar in range(2):
                re = gains[2 * polar : 2 * polar + 1]
                im = gains[2 * polar + 1 : 2 * polar + 2]
                w_re = (re * cosine - im * sine).astype(jnp.bfloat16)
                minus_im = (re * sine + im * cosine).astype(jnp.bfloat16)
                lhs = jnp.concatenate(
                    [
                        jnp.concatenate([w_re, minus_im], 1),
                        jnp.concatenate([-minus_im, w_re], 1),
                    ],
                    0,
                )
                y = jnp.dot(lhs, rhs_ref[polar], preferred_element_type=jnp.float32)
                y = y * y
                y = y[:rows] + y[rows:]
                power = y if power is None else power + y
            power = (power[:, :half] + power[:, half:]) * 0.5
            out_ref[pl.ds(origin + block * rows, rows), :] = power.astype(jnp.bfloat16)

    detect(near_ref, 0, SPLITS)
    far_copy.wait()
    detect(far_ref, near, SPLITS)


def fit_and_detect(cal, near, far, rhs):
    total, _, half_stations = cal.shape
    stations = near.shape[2]
    beams = near.shape[1] + far.shape[1]
    samples = rhs.shape[2]
    state = pltpu.VMEM((total, 8, half_stations), jnp.float32)
    return pl.pallas_call(
        beam_kernel,
        out_shape=(
            jax.ShapeDtypeStruct((beams, samples // 2), jnp.bfloat16),
            jax.ShapeDtypeStruct((4, stations), jnp.float32),
        ),
        in_specs=[VMEM_SPEC, VMEM_SPEC, HBM_SPEC, VMEM_SPEC],
        out_specs=(VMEM_SPEC, VMEM_SPEC),
        scratch_shapes=[pltpu.VMEM(far.shape, jnp.float32)]
        + [state] * 4
        + [pltpu.SemaphoreType.DMA((1,))],
        compiler_params=pltpu.CompilerParams(vmem_limit_bytes=GRANT - 24 * MIB),
        name="beams",
    )(cal, near, in_hbm(far), rhs)


def body(voltages, cal_num, cal_weight, flags, positions, directions, pointing):
    devices = lax.axis_size("chan")
    assert voltages.shape[0] == 1
    total = devices
    packed = pack(cal_num[0], cal_weight[0], flags, devices)
    cal = lax.all_to_all(packed, "chan", 0, 0, tiled=True)
    near, far, rhs = phasors(voltages[0], positions, directions, pointing[None, :], total)
    power, fitted = fit_and_detect(cal, near, far, rhs)
    moved = lax.all_to_all(power, "chan", 0, 0, tiled=True)
    beams = power.shape[0] // devices
    beam_power = jnp.transpose(moved.reshape(devices, beams, power.shape[1]), (1, 0, 2))
    return beam_power, fitted[None]


def solution(mesh):
    return jax.shard_map(
        body,
        mesh=mesh,
        in_specs=(
            P(("group", "chan"), None, None, None),
            P(("group", "chan"), None, None),
            P(("group", "chan"), None, None),
            P(("group", "chan"), None),
            P(),
            P(),
            P("group"),
        ),
        out_specs=(P(("group", "chan"), None, None), P(("group", "chan"), None, None)),
        check_vma=False,
    )
```

```python
import functools

import jax
import jax.numpy as jnp
import numpy as np
from jax import lax
from jax.experimental import pallas as pl
from jax.experimental.pallas import tpu as pltpu
from jax.sharding import PartitionSpec as P

ITERS = 8
ORDER = 4
PENALTY = 2.0
RIDGE = 1.0
MIB = 1 << 20
LANES = 128
NEAR = 4
SPLITS = 1
GRANT = 67_000_000


def legendre(place):
    return [
        1.0,
        place,
        0.5 * (3.0 * place * place - 1.0),
        0.5 * (5.0 * place * place * place - 3.0 * place),
    ]


def basis_table(total):
    place = np.float32(2.0) * (np.arange(total, dtype=np.float32) + np.float32(0.5)) / np.float32(
        total
    ) - np.float32(1.0)
    return np.stack([np.broadcast_to(np.float32(v), place.shape) for v in legendre(place)], 1)


HBM_SPEC = pl.BlockSpec(memory_space=pltpu.HBM)
VMEM_SPEC = pl.BlockSpec(memory_space=pltpu.VMEM)


def in_hbm(x):
    return pltpu.with_memory_space_constraint(x, pltpu.HBM)


def start(source, target, semaphore):
    copy = pltpu.make_async_copy(source, target, semaphore)
    copy.start()
    return copy


NUM_MOST = 6.0
WEIGHT_MOST = 5.0
LEVELS = 32767.0
STEPS = 14


def stacked(x):
    half = x.shape[1] // 2
    return jnp.concatenate([x[:, :half], x[:, half:]], 0)


def even_rows(x):
    return lax.broadcasted_iota(jnp.int32, x.shape, 0) % 2 == 0


def beside(x, even):
    return jnp.where(even, pltpu.roll(x, 7, 0), pltpu.roll(x, 1, 0))


def pack_kernel(num_hbm, weight_hbm, flag_hbm, out_ref, num_ref, weight_ref, flag_ref, sems):
    copies = [
        start(num_hbm, num_ref, sems.at[0]),
        start(weight_hbm, weight_ref, sems.at[1]),
        start(flag_hbm, flag_ref, sems.at[2]),
    ]
    for copy in copies:
        copy.wait()
    mask = flag_ref[...].astype(jnp.float32)
    num = stacked(num_ref[...] * mask)
    weight = weight_ref[...] * mask
    weight = stacked(jnp.concatenate([weight[0:1], weight[0:1], weight[1:2], weight[1:2]], 0))
    even = even_rows(num)
    size = jnp.abs(num)
    size = jnp.maximum(size, beside(size, even))
    scale = jnp.ones_like(size)
    inverse = jnp.ones_like(size)
    for power in range(1, STEPS + 1):
        larger = size > NUM_MOST * 2.0 ** (power - 1 - STEPS)
        scale = jnp.where(larger, 2.0**power, scale)
        inverse = jnp.where(larger, 2.0**-power, inverse)
    coded = jnp.round(num * inverse * (LEVELS * 2.0**STEPS / NUM_MOST))
    coded = jnp.clip(coded, -LEVELS, LEVELS)
    level = jnp.clip(jnp.round(weight * (LEVELS / WEIGHT_MOST)), 0.0, LEVELS)
    block = jnp.concatenate([coded, jnp.where(even, level, scale)], 0)
    block = block.astype(jnp.int32).astype(out_ref.dtype)
    for peer in range(out_ref.shape[0]):
        out_ref[peer] = block


def unpack(block):
    block = block.astype(jnp.int32).astype(jnp.float32)
    coded, side = block[0:8], block[8:16]
    even = even_rows(side)
    weight = jnp.where(even, side, pltpu.roll(side, 1, 0)) * (WEIGHT_MOST / LEVELS)
    scale = jnp.where(even, pltpu.roll(side, 7, 0), side)
    return coded * (scale * (NUM_MOST / (LEVELS * 2.0**STEPS))), weight


def pack(cal_num, cal_weight, flags, devices):
    stations = cal_num.shape[1]
    return pl.pallas_call(
        pack_kernel,
        out_shape=jax.ShapeDtypeStruct((devices, 16, stations // 2), jnp.int16),
        in_specs=[HBM_SPEC] * 3,
        out_specs=VMEM_SPEC,
        scratch_shapes=[
            pltpu.VMEM(cal_num.shape, jnp.float32),
            pltpu.VMEM(cal_weight.shape, jnp.float32),
            pltpu.VMEM(flags.shape, jnp.int32),
            pltpu.SemaphoreType.DMA((3,)),
        ],
        compiler_params=pltpu.CompilerParams(vmem_limit_bytes=GRANT),
        name="pack",
    )(cal_num, cal_weight, flags)


def fit_polynomials():
    nodes = np.cos(np.pi * (np.arange(400) + 0.5) / 400) * 0.5
    square = nodes * nodes
    safe = np.sinc(nodes) * np.pi
    chebyshev = np.polynomial.chebyshev.Chebyshev
    sine = chebyshev.fit(square, safe, 4, domain=[0, 0.25])
    cosine = chebyshev.fit(square, np.cos(np.pi * nodes), 5, domain=[0, 0.25])
    to_power = lambda c: c.convert(kind=np.polynomial.Polynomial).coef * np.sqrt(2.0)
    return [float(np.float32(v)) for v in to_power(sine)], [
        float(np.float32(v)) for v in to_power(cosine)
    ]


def horner(coefficients, x):
    value = coefficients[-1]
    for c in coefficients[-2::-1]:
        value = value * x + c
    return value


def thirds(x):
    high = x.astype(jnp.bfloat16).astype(jnp.float32)
    middle = (x - high).astype(jnp.bfloat16).astype(jnp.float32)
    return [high, middle, x - high - middle]


def phasor_kernel(
    rows, blocks, total, volts_hbm, pos_hbm, dir_hbm, point_hbm, near_ref, far_hbm, rhs_ref,
    volts_ref, pos_ref, dir_ref, point_ref, far_ref, dirs, sems, out_sems,
):
    incoming = [
        start(point_hbm, point_ref, sems.at[0]),
        start(dir_hbm, dir_ref, sems.at[1]),
        start(pos_hbm, pos_ref, sems.at[2]),
        start(volts_hbm, volts_ref, sems.at[3]),
    ]
    table = dir_ref.shape[1]
    beams = point_ref.shape[1]
    stations = pos_ref.shape[1]
    samples = volts_ref.shape[1]
    channel = lax.axis_index("chan").astype(jnp.float32)
    ratio = 1.0 + 0.3 * (channel + 0.5) / total
    for copy in incoming[:3]:
        copy.wait()

    parts = jnp.concatenate(thirds(dir_ref[...]) + [jnp.zeros_like(dir_ref[...])], 0)
    groups = table // LANES
    stack = jnp.concatenate([parts[:, g * LANES : (g + 1) * LANES] for g in range(groups)], 0)
    point = point_ref[...]
    hot = (
        (lax.broadcasted_iota(jnp.int32, (LANES, beams), 0) == (point & (LANES - 1)))
        .astype(jnp.float32)
        .astype(jnp.bfloat16)
    )
    spots = jnp.dot(stack.astype(jnp.bfloat16), hot, preferred_element_type=jnp.float32)
    group = point // LANES
    found = jnp.where(group == 0, spots[0:8], 0.0)
    for g in range(1, groups):
        found = found + jnp.where(group == g, spots[8 * g : 8 * g + 8], 0.0)
    dirs[...] = jnp.transpose(jnp.concatenate([found] * 4, 0)).astype(jnp.bfloat16)
    place = pos_ref[...] * ratio
    places = jnp.concatenate(
        [jnp.concatenate([third] * 3 + [jnp.zeros_like(third)], 0) for third in thirds(place)]
        + [jnp.zeros((8, stations), jnp.float32)],
        0,
    ).astype(jnp.bfloat16)

    outgoing = []
    incoming[3].wait()
    half = samples // 2
    row = lax.broadcasted_iota(jnp.int32, (samples, samples), 0)
    column = lax.broadcasted_iota(jnp.int32, (samples, samples), 1)
    source = jnp.where(column < half, 2 * column, 2 * (column - half) + 1)
    spread = (row == source).astype(jnp.float32).astype(jnp.bfloat16)
    for polar in range(2):
        turned = lax.dot_general(
            volts_ref[polar], spread, (((0,), (0,)), ((), ())), preferred_element_type=jnp.float32
        )
        rhs_ref[polar] = turned.astype(jnp.bfloat16)
    sine_c, cosine_c = fit_polynomials()
    near = near_ref.shape[1]
    per_block = (beams - near) // blocks

    def fill(target, first, origin, count):
        for step in range(count // rows):
            turns = jnp.dot(
                dirs[pl.ds(origin + first + step * rows, rows), :],
                places,
                preferred_element_type=jnp.float32,
            )
            x = turns - jnp.round(turns)
            square = x * x
            s = x * horner(sine_c, square)
            c = horner(cosine_c, square)
            at = pl.ds(first + step * rows, rows)
            target[0, at, :] = 1.0 - s * s
            target[1, at, :] = s * c

    for block in range(blocks):
        fill(far_ref, block * per_block, near, per_block)
        part = pl.ds(block * per_block, per_block)
        outgoing.append(start(far_ref.at[:, part], far_hbm.at[:, part], out_sems.at[block]))
    fill(near_ref, 0, 0, near)
    for copy in outgoing:
        copy.wait()


def phasors(volts, positions, directions, pointing, total):
    beams = pointing.shape[1]
    stations = positions.shape[1]
    samples = volts.shape[1]
    blocks = 4
    near = beams * NEAR // 8
    far = (2, beams - near, stations)
    rhs = (2, 2 * stations, samples)
    return pl.pallas_call(
        functools.partial(phasor_kernel, 64, blocks, total),
        out_shape=(
            jax.ShapeDtypeStruct((2, near, stations), jnp.float32),
            pltpu.HBM(far, jnp.float32),
            jax.ShapeDtypeStruct(rhs, jnp.bfloat16),
        ),
        in_specs=[HBM_SPEC] * 4,
        out_specs=(VMEM_SPEC, HBM_SPEC, VMEM_SPEC),
        scratch_shapes=[
            pltpu.VMEM(volts.shape, volts.dtype),
            pltpu.VMEM(positions.shape, jnp.float32),
            pltpu.VMEM(directions.shape, jnp.float32),
            pltpu.VMEM(pointing.shape, jnp.int32),
            pltpu.VMEM(far, jnp.float32),
            pltpu.VMEM((beams, 32), jnp.bfloat16),
            pltpu.SemaphoreType.DMA((4,)),
            pltpu.SemaphoreType.DMA((blocks,)),
        ],
        compiler_params=pltpu.CompilerParams(vmem_limit_bytes=GRANT - 24 * MIB),
        cost_estimate=pl.CostEstimate(
            flops=60 * beams * stations, bytes_accessed=8 * MIB, transcendentals=0
        ),
        name="phasors",
    )(*map(in_hbm, (volts, positions, directions, pointing)))


def invert_small(left):
    order = len(left)
    unit = jnp.ones_like(left[0][0])
    nothing = jnp.zeros_like(unit)
    right = [[unit if r == c else nothing for c in range(order)] for r in range(order)]
    for pivot in range(order):
        factor = 1.0 / left[pivot][pivot]
        left[pivot] = [entry * factor for entry in left[pivot]]
        right[pivot] = [entry * factor for entry in right[pivot]]
        for r in range(order):
            if r != pivot:
                scale = left[r][pivot]
                left[r] = [a - scale * b for a, b in zip(left[r], left[pivot])]
                right[r] = [a - scale * b for a, b in zip(right[r], right[pivot])]
    return right


def combine(weights, values):
    total = None
    for w, v in zip(weights, values):
        term = v if isinstance(w, float) and w == 1.0 else w * v
        total = term if total is None else total + term
    return total


def solve(cal_ref, target, keep, lean, history):
    total = cal_ref.shape[0]
    half = cal_ref.shape[2]
    table = basis_table(total)
    pairs = [(c, total - 1 - c, [float(v) for v in table[c]]) for c in range(total // 2)]

    def gather_sums(sums, first, second, line):
        even, odd = first + second, first - second
        terms = (even, line[1] * odd, line[2] * even, line[3] * odd)
        return [t if s is None else s + t for s, t in zip(sums, terms)]

    gram = [[None] * ORDER for _ in range(ORDER)]
    sums = [None] * ORDER
    for first, second, line in pairs:
        masks, values = [], []
        for c in (first, second):
            num, weight = unpack(cal_ref[c])
            mask = jnp.where(weight > 0.0, 1.0, 0.0)
            inverse = 1.0 / (weight + PENALTY)
            gain = mask * (PENALTY * inverse)
            value = num * inverse
            target[c] = value
            history[c] = value
            keep[c] = mask - gain
            lean[c] = 2.0 * gain - mask
            masks.append(mask)
            values.append(value)
        sums = gather_sums(sums, *values, line)
        even, odd = masks[0] + masks[1], masks[0] - masks[1]
        for k in range(ORDER):
            for j in range(k, ORDER):
                term = (even if (k + j) % 2 == 0 else odd) * (line[k] * line[j])
                gram[k][j] = term if gram[k][j] is None else gram[k][j] + term
    for k in range(ORDER):
        gram[k][k] = gram[k][k] + RIDGE
        for j in range(k):
            gram[k][j] = gram[j][k]
    inverse = invert_small(gram)
    coefficients = tuple(combine(inverse[k], sums) for k in range(ORDER))

    def sweep(_, coefficients):
        sums = [None] * ORDER
        for first, second, line in pairs:
            even = coefficients[0] + line[2] * coefficients[2]
            odd = line[1] * coefficients[1] + line[3] * coefficients[3]
            values = []
            for c, fitted in ((first, even + odd), (second, even - odd)):
                u = (target[c] + keep[c] * history[c]) + lean[c] * fitted
                history[c] = u
                values.append(u)
            sums = gather_sums(sums, *values, line)
        return tuple(combine(inverse[k], sums) for k in range(ORDER))

    coefficients = lax.fori_loop(1, ITERS, sweep, coefficients)
    channel = lax.axis_index("chan").astype(jnp.float32)
    place = 2.0 * (channel + 0.5) / total - 1.0
    return combine(legendre(place), coefficients)


def beam_kernel(
    cal_ref, near_ref, far_hbm, rhs_ref, out_ref, fitted_ref,
    far_ref, target, keep, lean, history, sems,
):
    near, stations = near_ref.shape[1:]
    half = rhs_ref.shape[2] // 2
    far_copy = start(far_hbm, far_ref, sems.at[0])
    fitted = solve(cal_ref, target, keep, lean, history)
    fitted_ref[:, : stations // 2] = fitted[0:4]
    fitted_ref[:, stations // 2 :] = fitted[4:8]
    _, own = unpack(cal_ref[lax.axis_index("chan")])
    dense = fitted * jnp.where(own > 0.0, stations ** (-0.5), 0.0)
    gains = jnp.concatenate([dense[0:4], dense[4:8]], 1)

    def detect(phase_ref, origin, splits):
        rows = phase_ref.shape[1] // splits
        for block in range(splits):
            part = pl.ds(block * rows, rows)
            cosine = phase_ref[0, part]
            sine = phase_ref[1, part]
            power = None
            for polar in range(2):
                re = gains[2 * polar : 2 * polar + 1]
                im = gains[2 * polar + 1 : 2 * polar + 2]
                w_re = (re * cosine - im * sine).astype(jnp.bfloat16)
                minus_im = (re * sine + im * cosine).astype(jnp.bfloat16)
                lhs = jnp.concatenate(
                    [
                        jnp.concatenate([w_re, minus_im], 1),
                        jnp.concatenate([-minus_im, w_re], 1),
                    ],
                    0,
                )
                y = jnp.dot(lhs, rhs_ref[polar], preferred_element_type=jnp.float32)
                y = y * y
                y = y[:rows] + y[rows:]
                power = y if power is None else power + y
            power = (power[:, :half] + power[:, half:]) * 0.5
            out_ref[pl.ds(origin + block * rows, rows), :] = power.astype(jnp.bfloat16)

    detect(near_ref, 0, SPLITS)
    far_copy.wait()
    detect(far_ref, near, SPLITS)


def fit_and_detect(cal, near, far, rhs):
    total, _, half_stations = cal.shape
    stations = near.shape[2]
    beams = near.shape[1] + far.shape[1]
    samples = rhs.shape[2]
    state = pltpu.VMEM((total, 8, half_stations), jnp.float32)
    return pl.pallas_call(
        beam_kernel,
        out_shape=(
            jax.ShapeDtypeStruct((beams, samples // 2), jnp.bfloat16),
            jax.ShapeDtypeStruct((4, stations), jnp.float32),
        ),
        in_specs=[VMEM_SPEC, VMEM_SPEC, HBM_SPEC, VMEM_SPEC],
        out_specs=(VMEM_SPEC, VMEM_SPEC),
        scratch_shapes=[pltpu.VMEM(far.shape, jnp.float32)]
        + [state] * 4
        + [pltpu.SemaphoreType.DMA((1,))],
        compiler_params=pltpu.CompilerParams(vmem_limit_bytes=GRANT - 24 * MIB),
        name="beams",
    )(cal, near, in_hbm(far), rhs)


def arrange_kernel(moved_ref, out_ref):
    out_ref[...] = jnp.swapaxes(moved_ref[...], 0, 1)


def arrange(moved):
    channels, beams, samples = moved.shape
    return pl.pallas_call(
        arrange_kernel,
        out_shape=jax.ShapeDtypeStruct((beams, channels, samples), moved.dtype),
        in_specs=[VMEM_SPEC],
        out_specs=VMEM_SPEC,
        compiler_params=pltpu.CompilerParams(vmem_limit_bytes=GRANT - 24 * MIB),
        name="arrange",
    )(moved)


def body(voltages, cal_num, cal_weight, flags, positions, directions, pointing):
    devices = lax.axis_size("chan")
    assert voltages.shape[0] == 1
    total = devices
    packed = pack(cal_num[0], cal_weight[0], flags, devices)
    cal = lax.all_to_all(packed, "chan", 0, 0, tiled=True)
    near, far, rhs = phasors(voltages[0], positions, directions, pointing[None, :], total)
    power, fitted = fit_and_detect(cal, near, far, rhs)
    moved = lax.all_to_all(power, "chan", 0, 0, tiled=True)
    beam_power = arrange(moved.reshape(devices, power.shape[0] // devices, power.shape[1]))
    return beam_power, fitted[None]


def solution(mesh):
    return jax.shard_map(
        body,
        mesh=mesh,
        in_specs=(
            P(("group", "chan"), None, None, None),
            P(("group", "chan"), None, None),
            P(("group", "chan"), None, None),
            P(("group", "chan"), None),
            P(),
            P(),
            P("group"),
        ),
        out_specs=(P(("group", "chan"), None, None), P(("group", "chan"), None, None)),
        check_vma=False,
    )
```
